256 devices in a mesh: leaf: 64 (over x, z, core), rhs: 4 (over y).
Axes of the slice: x: 4, y: 4, z: 8, core: 2. Of those that a mesh axis runs over, the one named last changes fastest.
Arguments:
- input_columns: float32 [8, 1024, 256], P('rhs', 'leaf'), may hold values from -6 to 6
- near_blocks: float32 [8192, 256, 256], P(('leaf', 'rhs')), may hold values from -0.25 to 0.25
- near_pairs: int32 [8192, 2], P(('leaf', 'rhs')), may hold values from -1 to 1023, as said below
- leaf_basis: float32 [1024, 64, 256], P(('leaf', 'rhs')), may hold values from -0.375 to 0.375
- local_transfer: float32 [1792, 64, 64], P('leaf'), may hold values from -0.5 to 0.5
- local_coupling: float32 [1792, 4, 64, 64], P('leaf'), may hold values from -0.4375 to 0.4375
- local_lists: int32 [1792, 4], P('leaf'), may hold values from -1 to 1023, as said below
- middle_transfer: float32 [128, 64, 64], P('leaf'), may hold values from -0.5 to 0.5
- middle_coupling: float32 [192, 4, 64, 64], P('leaf'), may hold values from -0.75 to 0.75
- middle_lists: int32 [192, 4], P('leaf'), may hold values from -1 to 127, as said below
- upper_transfer: float32 [126, 64, 64], replicated, may hold values from -0.5 to 0.5
- upper_coupling: float32 [64, 4, 64, 64], P('leaf'), may hold values from -1 to 1
- upper_lists: int32 [64, 4], P('leaf'), may hold values from -1 to 31, as said below
Outputs:
- first_product: float32 [8, 1024, 256], P(None, ('leaf', 'rhs'))
- second_product: float32 [8, 1024, 256], P(None, ('leaf', 'rhs'))
The draws below stay inside these ranges and needn't reach their ends.
Inputs may be any that keep to these rules, and one draw needn't show every extreme that they name: `near_pairs`: each slot holds (receiving leaf, source leaf). The 32 slots of each device along leaf+rhs belong to receiving leaves among that device's 4 leaves; live pairs come first, the remaining slots are -1 in both columns. The source leaf lies within 4 leaves of the receiving one. In every draw some device has all its slots live. `local_lists`: each entry is -1 (unused) or the number, among the clusters of the same level counted from 0 in leaf order, of a cluster whose number differs from the listing cluster's by 2 or 3; entries of one list differ. `middle_lists`: as for the local lists, at the level of the subtree roots and the level below it. `upper_lists`: row h lists for heap cluster h (level t with 2^t <= h < 2^(t+1), number h - 2^t) as for the local lists; rows 0 to 3 are -1.
All inputs are finite; a program needn't handle non-finite values.
Results may differ from the reference program's by a relative error of at most 0.0003.
Values sent between devices are 32-bit elements; how exact they have to be, the bound alone decides.
A program may use at most 128 MiB of HBM per device.

```python
import jax
import jax.numpy as jnp
from jax import lax

LEAF_SIZE = 256
BASIS_RANK = 64
LIST_SLOTS = 4
NEAR_REACH = 4
LEAF_DEV = 16
SUBTREES = 64
LEAVES = 1024
COLUMNS = 8
LEAF_SHARD = 4
NEAR_SHARD = 32
NEAR_SLOTS = 8192
LOCAL_NODES = 1792
MID_MOVED = 128
MID_COUPLED = 192
TOP_MOVED = 126


def make_lists(key, position, level_size):
    rows_total = position.shape[0]
    offset_table = jnp.array([-3, -2, 2, 3], dtype=jnp.int32)
    rotation = jax.random.randint(jax.random.fold_in(key, 11), (rows_total,), 0, 4)
    slot_order = (jnp.arange(LIST_SLOTS, dtype=jnp.int32)[None, :] + rotation[:, None]) % 4
    candidate = position[:, None] + jnp.take(offset_table, slot_order)
    keep_entry = jax.random.randint(jax.random.fold_in(key, 12), (rows_total, LIST_SLOTS), 0, 4) > 0
    keep_entry = keep_entry | (candidate == level_size[:, None] - 1)
    inside = (candidate >= 0) & (candidate < level_size[:, None])
    return jnp.where(keep_entry & inside, candidate, -1).astype(jnp.int32)


def draw_local_lists(key, part):
    per_tree = 2 * LEAF_DEV - 4
    subtrees = LOCAL_NODES // per_tree
    node_index = jnp.arange(LOCAL_NODES, dtype=jnp.int32)
    subtree = node_index // per_tree
    within = node_index % per_tree
    sublevel = jnp.zeros((LOCAL_NODES,), jnp.int32)
    for exponent in range(1, LEAF_DEV.bit_length() - 2):
        sublevel = sublevel + (within >= 4 * (2 ** exponent - 1)).astype(jnp.int32)
    scale_up = jnp.power(2, sublevel).astype(jnp.int32)
    amount = 4 * scale_up
    position = subtree * amount + within - 4 * (scale_up - 1)
    return make_lists(key, position, subtrees * amount)


def draw_middle_lists(key, part):
    node_index = jnp.arange(MID_COUPLED, dtype=jnp.int32)
    subtree = node_index // 3
    slot_kind = node_index % 3
    subtrees = MID_COUPLED // 3
    position = jnp.where(slot_kind == 0, subtree, 2 * subtree + slot_kind - 1)
    level_size = jnp.where(slot_kind == 0, subtrees, 2 * subtrees).astype(jnp.int32)
    return make_lists(key, position, level_size)


def draw_upper_lists(key, part):
    node_index = jnp.arange(SUBTREES, dtype=jnp.int32)
    level_start = jnp.ones((SUBTREES,), jnp.int32)
    for exponent in range(1, 16):
        level_start = jnp.where(node_index >= 2 ** exponent, 2 ** exponent, level_start)
    lists = make_lists(key, node_index - level_start, level_start)
    return jnp.where((node_index >= 4)[:, None], lists, -1).astype(jnp.int32)


def draw_near_pairs(key, part):
    shards = NEAR_SLOTS // NEAR_SHARD
    live_count = jax.random.randint(jax.random.fold_in(key, 21), (shards,), 2 * NEAR_SHARD // 3, NEAR_SHARD + 1)
    busiest = jax.random.randint(jax.random.fold_in(key, 23), (), 0, shards)
    live_count = jnp.where(jnp.arange(shards, dtype=jnp.int32) == busiest, NEAR_SHARD, live_count)
    slot_index = jnp.arange(NEAR_SLOTS, dtype=jnp.int32)
    shard_index = slot_index // NEAR_SHARD
    place_index = slot_index % NEAR_SHARD
    target = shard_index * LEAF_SHARD + jax.random.randint(jax.random.fold_in(key, 24), (NEAR_SLOTS,), 0, LEAF_SHARD)
    shifted = jax.random.randint(jax.random.fold_in(key, 25), (NEAR_SLOTS,), -NEAR_REACH, NEAR_REACH + 1)
    source = jnp.clip(target + shifted, 0, LEAVES - 1)
    is_alive = place_index < jnp.take(live_count, shard_index)
    return jnp.stack([jnp.where(is_alive, target, -1), jnp.where(is_alive, source, -1)], axis=1).astype(jnp.int32)


def steps_of(own_key, extent, cuts, least, high):
    def one(dim, parts):
        heights = jax.random.uniform(jax.random.fold_in(jax.random.fold_in(own_key, 6), dim), (parts,), jnp.float32, least / len(cuts), high / len(cuts))
        return jnp.repeat(jnp.exp(heights), extent[dim] // parts).reshape((-1,) + (1,) * (len(extent) - dim - 1))

    gain = one(*cuts[0])
    for cut in cuts[1:]:
        gain = gain * one(*cut)
    return gain


def centred(rng, extent, spread, limit, cuts=(), kind=jnp.bfloat16):
    level = steps_of(rng, extent, cuts, -0.22, 0.18) if cuts else 1.0
    drawn = jax.random.normal(rng, extent, jnp.float32) * spread * level
    return jnp.minimum(jnp.maximum(drawn, -limit), limit).astype(kind)


def setup_inputs(seed: int = 0) -> dict:
    streams_of = jax.random.split(jax.random.key(seed), 14)
    input_columns = centred(streams_of[0], (COLUMNS, LEAVES, LEAF_SIZE), 1.0, 6.0, ((0, 4), (1, 64)), jnp.float32)
    near_blocks = centred(streams_of[1], (NEAR_SLOTS, LEAF_SIZE, LEAF_SIZE), (2 * LEAF_SIZE) ** -0.5, 0.25, ((0, 256),), jnp.float32)
    near_pairs = draw_near_pairs(jax.random.fold_in(streams_of[13], 71), 0)
    leaf_basis = centred(streams_of[3], (LEAVES, BASIS_RANK, LEAF_SIZE), LEAF_SIZE ** -0.5, 0.375, ((0, 256),), jnp.float32)
    local_transfer = centred(streams_of[4], (LOCAL_NODES, BASIS_RANK, BASIS_RANK), (2 * BASIS_RANK) ** -0.5, 0.5, ((0, 64),), jnp.float32)
    local_coupling = centred(streams_of[5], (LOCAL_NODES, LIST_SLOTS, BASIS_RANK, BASIS_RANK), (3 * BASIS_RANK) ** -0.5, 0.4375, ((0, 64),), jnp.float32)
    local_lists = draw_local_lists(jax.random.fold_in(streams_of[13], 71), 0)
    middle_transfer = centred(streams_of[7], (MID_MOVED, BASIS_RANK, BASIS_RANK), (2 * BASIS_RANK) ** -0.5, 0.5, ((0, 64),), jnp.float32)
    middle_coupling = centred(streams_of[8], (MID_COUPLED, LIST_SLOTS, BASIS_RANK, BASIS_RANK), BASIS_RANK ** -0.5, 0.75, ((0, 64),), jnp.float32)
    middle_lists = draw_middle_lists(jax.random.fold_in(streams_of[13], 71), 0)
    upper_transfer = centred(streams_of[10], (TOP_MOVED, BASIS_RANK, BASIS_RANK), (2 * BASIS_RANK) ** -0.5, 0.5, (), jnp.float32)
    upper_coupling = centred(streams_of[11], (SUBTREES, LIST_SLOTS, BASIS_RANK, BASIS_RANK), (BASIS_RANK // 2) ** -0.5, 1.0, ((0, 64),), jnp.float32)
    upper_lists = draw_upper_lists(jax.random.fold_in(streams_of[13], 71), 0)
    return {"input_columns": input_columns, "near_blocks": near_blocks, "near_pairs": near_pairs, "leaf_basis": leaf_basis, "local_transfer": local_transfer, "local_coupling": local_coupling, "local_lists": local_lists, "middle_transfer": middle_transfer, "middle_coupling": middle_coupling, "middle_lists": middle_lists, "upper_transfer": upper_transfer, "upper_coupling": upper_coupling, "upper_lists": upper_lists}


highest = lax.Precision.HIGHEST


def lift_level(matrices, vectors):
    moved = jnp.einsum('nab,cna->cnb', matrices, vectors, precision=highest)
    return moved.reshape(moved.shape[0], moved.shape[1] // 2, 2, moved.shape[2]).sum(axis=2)


def couple_lists(blocks, positions, valid, table):
    clipped = jnp.clip(positions, 0, table.shape[1] - 1).astype(jnp.int32)
    picked = jnp.take(table, clipped, axis=1)
    picked = picked * valid.astype(table.dtype)[None, :, :, None]
    return jnp.einsum('nkab,cnkb->cna', blocks, picked, precision=highest)


def level_transfer(tree_level, top_depth, tree_data):
    local_transfer, middle_transfer, upper_transfer = tree_data[0], tree_data[3], tree_data[6]
    if tree_level <= top_depth:
        return upper_transfer[2 ** tree_level - 2:2 ** (tree_level + 1) - 2]
    if tree_level == top_depth + 1:
        return middle_transfer
    sublevel = tree_level - top_depth - 2
    amount = 4 * 2 ** sublevel
    offset = 4 * (2 ** sublevel - 1)
    per_tree = 2 * LEAF_DEV - 4
    shaped = local_transfer.reshape(SUBTREES, per_tree, BASIS_RANK, BASIS_RANK)[:, offset:offset + amount]
    return shaped.reshape(SUBTREES * amount, BASIS_RANK, BASIS_RANK)


def level_coupling(tree_level, top_depth, tree_data):
    local_coupling, local_lists = tree_data[1], tree_data[2]
    middle_coupling, middle_lists = tree_data[4], tree_data[5]
    upper_coupling, upper_lists = tree_data[7], tree_data[8]
    if tree_level < top_depth:
        lower_end = 2 ** tree_level
        return upper_coupling[lower_end:2 * lower_end], upper_lists[lower_end:2 * lower_end]
    if tree_level <= top_depth + 1:
        blocks = middle_coupling.reshape(SUBTREES, 3, LIST_SLOTS, BASIS_RANK, BASIS_RANK)
        entries = middle_lists.reshape(SUBTREES, 3, LIST_SLOTS)
        if tree_level == top_depth:
            return blocks[:, 0], entries[:, 0]
        return (blocks[:, 1:].reshape(2 * SUBTREES, LIST_SLOTS, BASIS_RANK, BASIS_RANK),
                entries[:, 1:].reshape(2 * SUBTREES, LIST_SLOTS))
    sublevel = tree_level - top_depth - 2
    amount = 4 * 2 ** sublevel
    offset = 4 * (2 ** sublevel - 1)
    per_tree = 2 * LEAF_DEV - 4
    blocks = local_coupling.reshape(SUBTREES, per_tree, LIST_SLOTS, BASIS_RANK, BASIS_RANK)[:, offset:offset + amount]
    entries = local_lists.reshape(SUBTREES, per_tree, LIST_SLOTS)[:, offset:offset + amount]
    return (blocks.reshape(SUBTREES * amount, LIST_SLOTS, BASIS_RANK, BASIS_RANK),
            entries.reshape(SUBTREES * amount, LIST_SLOTS))


def apply_matrix(vectors, near_blocks, near_pairs, leaf_basis, tree_data):
    top_depth = SUBTREES.bit_length() - 1
    leaf_level = top_depth + LEAF_DEV.bit_length() - 1
    columns_here = vectors.shape[0]
    upward = {leaf_level: jnp.einsum('gki,rgi->rgk', leaf_basis, vectors, precision=highest)}
    for tree_level in range(leaf_level, 0, -1):
        upward[tree_level - 1] = lift_level(level_transfer(tree_level, top_depth, tree_data), upward[tree_level])
    downward = jnp.zeros((columns_here, 1, BASIS_RANK), jnp.float32)
    for tree_level in range(1, leaf_level + 1):
        matrices = level_transfer(tree_level, top_depth, tree_data)
        downward = jnp.einsum('nab,cnb->cna', matrices, jnp.repeat(downward, 2, axis=1), precision=highest)
        if tree_level >= 2:
            blocks, entries = level_coupling(tree_level, top_depth, tree_data)
            downward = downward + couple_lists(blocks, entries, entries >= 0, upward[tree_level])
    far_part = jnp.einsum('gki,rgk->rgi', leaf_basis, downward, precision=highest)
    shards = NEAR_SLOTS // NEAR_SHARD

    def shard_terms(pieces):
        blocks, pairs = pieces
        sources = jnp.take(vectors, jnp.clip(pairs[:, 1], 0, LEAVES - 1).astype(jnp.int32), axis=1)
        return jnp.einsum('pij,rpj->pri', blocks, sources, precision=highest)

    terms = lax.map(shard_terms, (near_blocks.reshape(shards, NEAR_SHARD, LEAF_SIZE, LEAF_SIZE),
                                  near_pairs.reshape(shards, NEAR_SHARD, 2)))
    terms = terms.reshape(NEAR_SLOTS, columns_here, LEAF_SIZE)
    targets = jnp.where(near_pairs[:, 0] >= 0, near_pairs[:, 0], LEAVES).astype(jnp.int32)
    near_part = jax.ops.segment_sum(terms, targets, num_segments=LEAVES + 1)[:LEAVES].transpose(1, 0, 2)
    return near_part + far_part


def reference(input_columns, near_blocks, near_pairs, leaf_basis, local_transfer, local_coupling, local_lists,
              middle_transfer, middle_coupling, middle_lists, upper_transfer, upper_coupling, upper_lists):
    tree_data = (local_transfer, local_coupling, local_lists, middle_transfer, middle_coupling, middle_lists,
                 upper_transfer, upper_coupling, upper_lists)
    first_product = apply_matrix(input_columns, near_blocks, near_pairs, leaf_basis, tree_data)
    second_product = apply_matrix(first_product, near_blocks, near_pairs, leaf_basis, tree_data)
    return first_product, second_product
```

```python
import jax
import jax.numpy as jnp
from jax import lax
from jax.experimental import pallas as pl
from jax.experimental.pallas import tpu as pltpu
from jax.sharding import PartitionSpec as P

F32 = jnp.float32
BF16 = jnp.bfloat16
MESH = pl.DeviceIdType.MESH
NN = (((1,), (0,)), ((), ()))
NT = (((1,), (1,)), ((), ()))
XY = [(i, k) for i in range(4) for k in range(4) if (i, k) != (0, 0)]
XY_ORDER = sorted(XY, key=lambda s: -(min(s[0], 4 - s[0]) + min(s[1], 4 - s[1])))
ZC_ORDER = [(4, 0), (4, 1), (3, 0), (3, 1), (5, 0), (5, 1), (2, 0), (2, 1), (6, 0), (6, 1), (1, 0), (1, 1), (7, 0), (7, 1), (0, 1)]
NEAR_D = (1, -1, 2, -2, 3, -3, 4, -4, 8, -8)


def stacked(x):
    high = x.astype(BF16).astype(F32)
    return jnp.concatenate([high, x - high], axis=0).astype(BF16)


def parts(w):
    high = w.astype(BF16)
    return high, (w - high.astype(F32)).astype(BF16)


def dot(x, w, dims):
    return lax.dot_general(x, w, dims, preferred_element_type=F32)


def mm_parts(xs, high, low, dims):
    y = dot(xs, high, dims) + dot(xs, low, dims)
    rows = xs.shape[0] // 2
    return y[:rows] + y[rows:]


def mm(x, w, dims):
    return mm_parts(stacked(x), *parts(w), dims)


def left_lanes(shape):
    return lax.broadcasted_iota(jnp.int32, shape, len(shape) - 1) < 64


def swap(x):
    return pltpu.roll(x, 64, x.ndim - 1)


def kernel(
    pairs, local_lists, middle_lists, upper_lists,
    columns, near_hbm, basis_hbm, lt_hbm, lc_hbm, mt_hbm, mc_hbm, ut_hbm, uc_hbm,
    first_hbm, second_hbm,
    vin, vlf, vnext, near, basis, e10, e9, e8, e7, k10, k9, k8, k7, k6, ut, uc,
    dsend, dbuf, abuf, ahigh, alow, wup, q6s, q7s, q8s,
    halo_0, halo_1, xybuf, agsend, agbuf, c7_0, c7_1, acc, outs,
    load_sem, in_send, in_recv, edge_send, edge_recv, d_send, d_recv,
    xy_send, xy_recv, halo_send, halo_recv, ag_send, ag_recv, c7_send, c7_recv, v_send, v_recv, out_sem,
):
    halo, c7buf = (halo_0, halo_1), (c7_0, c7_1)
    g = lax.axis_index("leaf")
    q = lax.axis_index("rhs")
    d = 4 * g + q
    gx = g // 16
    zc = lax.rem(g, 16)
    gz, gc = zc // 2, lax.rem(zc, 2)

    def linear(k):
        e = lax.rem(d + k + 256, 256)
        return (e // 4, lax.rem(e, 4))

    def group(k):
        return lax.rem(g + k + 64, 64)

    def xy(i, k):
        return (lax.rem(gx + i, 4) * 16 + zc, lax.rem(q + k, 4))

    def zcs(i, k):
        return (gx * 16 + lax.rem(gz + i, 8) * 2 + lax.rem(gc + k, 2), q)

    loads = []

    def load(src, dst):
        c = pltpu.make_async_copy(src, dst, load_sem.at[len(loads)])
        c.start()
        loads.append(c)
        return c

    ld_own = load(columns, vin.at[pl.ds(2 * q, 2), 8:24])
    ld_uc = load(uc_hbm.at[0], uc)
    ld_basis = load(basis_hbm, basis)
    ld_e = [
        load(lt_hbm.at[pl.ds(12 + 4 * q, 4)], e10),
        load(lt_hbm.at[pl.ds(4 + 2 * q, 2)], e9),
        load(lt_hbm.at[q], e8),
        load(mt_hbm.at[q // 2], e7),
    ]
    ld_near = load(near_hbm, near)
    ld_k = [
        load(lc_hbm.at[pl.ds(12 + 4 * q, 4)], k10),
        load(lc_hbm.at[pl.ds(4 + 2 * q, 2)], k9),
        load(lc_hbm.at[q], k8),
        load(mc_hbm.at[1 + q // 2], k7),
        load(mc_hbm.at[0], k6),
    ]
    ld_ut = load(ut_hbm, ut)

    level = 2 + (g >= 8).astype(jnp.int32) + (g >= 16).astype(jnp.int32) + (g >= 32).astype(jnp.int32)
    count = jnp.where(g >= 32, 2, jnp.where(g >= 16, 4, jnp.where(g >= 8, 8, jnp.where(g >= 4, 16, 0))))
    start = jnp.where(g >= 32, 32, jnp.where(g >= 16, 16, jnp.where(g >= 8, 8, 4)))
    own_number = g - start
    first_below = own_number * count
    own_inside = jnp.where((g >= first_below) & (g < first_below + count), 1, 0)
    barrier = pltpu.get_barrier_semaphore()

    def greet(device):
        pl.semaphore_signal(barrier, inc=1, device_id=device, device_id_type=MESH)

    owners = [2**t + g // 2 ** (6 - t) for t in range(2, 6)]
    for s in XY_ORDER:
        greet(xy(*s))
    for s in ZC_ORDER:
        greet(zcs(*s))
    for k in NEAR_D:
        greet(linear(k))
    for owner in owners:
        @pl.when(owner != g)
        def _():
            greet((owner, q))
    pl.semaphore_wait(barrier, 15 + 15 + len(NEAR_D) + count - own_inside)

    def remote(src, dst, ss, rs, device):
        c = pltpu.make_async_remote_copy(
            src_ref=src, dst_ref=dst, send_sem=ss, recv_sem=rs, device_id=device, device_id_type=MESH
        )
        c.start()
        return c

    sent = []
    ins = []
    for k in (2, 1, 3):
        ins.append(
            remote(columns, vin.at[pl.ds(2 * q, 2), 8:24], in_send.at[k], in_recv.at[k], (g, lax.rem(q + k, 4)))
        )
    sent.append(remote(columns.at[:, 8:16], vin.at[pl.ds(2 * q, 2), 0:8], edge_send.at[0], edge_recv.at[0, q], (group(1), 0)))
    sent.append(remote(columns.at[:, 0:8], vin.at[pl.ds(2 * q, 2), 24:32], edge_send.at[1], edge_recv.at[1, q], (group(-1), 3)))

    def by_offset(blocks, entries, number):
        found = []
        for offset in (-3, -2, 2, 3):
            total = None
            for k in range(4):
                weight = jnp.where((entries[k] >= 0) & (entries[k] == number + offset), 1.0, 0.0)
                term = blocks[k] * weight
                total = term if total is None else total + term
            found.append(total)
        return (jnp.concatenate(found[:2], axis=1), jnp.concatenate(found[2:], axis=1))

    ld_uc.wait()
    low_half, high_half = by_offset(uc, [upper_lists[0, k] for k in range(4)], own_number)
    dsend[0] = low_half
    dsend[1] = high_half

    def give(i, carry):
        to = first_below + i

        @pl.when(to != g)
        def _():
            remote(dsend, dbuf.at[level - 2], d_send.at[i], d_recv.at[level - 2], (to, q))

        @pl.when(to == g)
        def _():
            pltpu.make_async_copy(dsend, dbuf.at[level - 2], d_recv.at[level - 2]).start()

        return carry

    lax.fori_loop(0, count, give, 0)

    for c in ld_e:
        c.wait()
    q8 = jnp.concatenate([mm(e10[l], e9[l // 2], NN) for l in range(4)], axis=0)
    q7 = mm(q8, e8[...], NN)
    q6 = mm(q7, e7[...], NN)
    q8s[...] = q8
    q7s[...] = q7
    q6s[...] = q6
    wup[:, 0:128] = jnp.concatenate([q7, q6], axis=1)
    wup[:, 128:256] = jnp.concatenate([q8, q8], axis=1)

    left = left_lanes((8, 128))
    quarter = lax.broadcasted_iota(jnp.int32, (8, 256), 1) // 64
    ld_own.wait()
    ld_basis.wait()
    for c in ins:
        c.wait_recv()
    sent.extend(ins)
    for i in range(16):
        vlf[4 + i] = vin[:, 8 + i, :]

    def climb(p, rows):
        wide = mm(rows, basis[...].reshape(256, 256), NT)
        c10 = jnp.zeros((8, 256), F32)
        for l in range(4):
            c10 = jnp.where(quarter == l, wide[8 * l : 8 * l + 8], c10)
        tops = mm(c10, wup[...], NN)
        xybuf[p, 0, 0] = tops[:, 0:128]
        halo[p][3, 3] = tops[:, 128:256]
        for i, k in XY_ORDER:
            xys[p].append(
                remote(xybuf.at[p, 0, 0], xybuf.at[p, i, k], xy_send.at[p, i, k], xy_recv.at[p, i, k], xy(i, k))
            )
        halo[p][3, 0] = c10[:, 0:128]
        halo[p][3, 1] = c10[:, 128:256]
        halo[p][3, 2] = jnp.concatenate(
            [mm(c10[:, 128 * j : 128 * j + 128], e10[2 * j : 2 * j + 2].reshape(128, 64), NN) for j in range(2)], axis=1
        )
        for k in (1, -1, 2, -2, 3, -3):
            tiles = pl.ds({1: 0, 2: 2, 3: 3}[abs(k)], {1: 4, 2: 2, 3: 1}[abs(k)])
            halos[p].append(
                remote(
                    halo[p].at[3, tiles], halo[p].at[3 - k, tiles], halo_send.at[p, 3 - k], halo_recv.at[p, 3 - k], linear(k)
                )
            )

    xys, halos, ags, c7s = ([], []), ([], []), ([], []), ([], [])

    def near_field(vectors, offset, least):
        def step(s, totals):
            target = pairs[0, s] - 4 * d
            source = jnp.clip(pairs[1, s] - offset, least, least + 11)
            term = mm(vectors[source], near[s], NT)
            return tuple(t + term * jnp.where(target == l, 1.0, 0.0) for l, t in enumerate(totals))

        zero = jnp.zeros((8, 256), F32)
        totals = lax.fori_loop(0, 32, step, (zero,) * 4, unroll=4)
        for l in range(4):
            acc[8 * l : 8 * l + 8] = totals[l]

    def half_of(tile, half):
        return jnp.where(half == 1, swap(tile), tile)[:, 0:64]

    def coupled(blocks, entries, pick):
        total = None
        for k in range(4):
            x = pick(entries[k]) * jnp.where(entries[k] >= 0, 1.0, 0.0)
            term = mm(x, blocks[k], NT)
            total = term if total is None else total + term
        return total

    def local_coupled(p):
        for c in halos[p]:
            c.wait_recv()
        sent.extend(halos[p])

        def pick10(entry):
            at = jnp.clip(entry - 4 * d + 12, 0, 27)
            return half_of(halo[p][at // 4, lax.rem(at, 4) // 2], lax.rem(at, 2))

        def pick9(entry):
            at = jnp.clip(entry - 2 * d + 6, 0, 13)
            return half_of(halo[p][at // 2, 2], lax.rem(at, 2))

        def pick8(entry):
            at = jnp.clip(entry - d + 3, 0, 6)
            return halo[p][at, 3][:, 0:64]

        z10 = [coupled(k10[l], [local_lists[k, 12 + 4 * q + l] for k in range(4)], pick10) for l in range(4)]
        z9 = [coupled(k9[j], [local_lists[k, 4 + 2 * q + j] for k in range(4)], pick9) for j in range(2)]
        z8 = coupled(k8, [local_lists[k, q] for k in range(4)], pick8)
        down = mm(z8, q8s[...], NT)
        below = [mm(z9[j], e10[2 * j : 2 * j + 2].reshape(128, 64), NT) for j in range(2)]
        return down + jnp.concatenate(
            [below[0] + jnp.concatenate(z10[0:2], axis=1), below[1] + jnp.concatenate(z10[2:4], axis=1)], axis=1
        )

    def middle(p):
        for c in xys[p]:
            c.wait_recv()
        sent.extend(xys[p])
        totals = []
        for x in range(4):
            i = lax.rem(gx - x + 4, 4)
            totals.append(xybuf[p, i, 0] + xybuf[p, i, 1] + xybuf[p, i, 2] + xybuf[p, i, 3])
        for j in range(2):
            agsend[p, j] = jnp.where(left, swap(totals[2 * j]), totals[2 * j + 1])
        for i, k in ZC_ORDER:
            ags[p].append(
                remote(agsend.at[p], agbuf.at[p, i, k], ag_send.at[p, i, k], ag_recv.at[p, i, k], zcs(i, k))
            )
        agbuf[p, 0, 0] = agsend[p]

        def own(y):
            return xybuf[p, 0, lax.rem(q - y + 4, 4)]

        c7buf[p][2] = jnp.where(left, own(0) + own(1), swap(own(2) + own(3)))
        for k in (1, -1, 2, -2):
            c7s[p].append(
                remote(c7buf[p].at[2], c7buf[p].at[2 - k], c7_send.at[p, 2 - k], c7_recv.at[p, 2 - k], (group(k), q))
            )

    def middle_coupled(p):
        for c in c7s[p]:
            c.wait_recv()
        sent.extend(c7s[p])

        def pick7(entry):
            at = jnp.clip(entry - 2 * g + 4, 0, 9)
            return half_of(c7buf[p][at // 2], lax.rem(at, 2))

        z7 = coupled(k7, [middle_lists[1 + q // 2, k] for k in range(4)], pick7)
        return mm(z7, q7s[...], NT)

    def upper_operator():
        offsets = {2: 0, 3: 2, 4: 6, 5: 14, 6: 30}
        lefts = left_lanes((64, 128))
        ld_ut.wait()

        def transfer(t):
            return ut[2**t - 2 + g // 2 ** (6 - t)]

        chain = {5: transfer(6)}
        for t in (4, 3, 2, 1, 0):
            chain[t] = mm(chain[t + 1], transfer(t + 1), NN)
        ld_k[4].wait()

        def add(t, lower, upper):
            number = g // 2 ** (6 - t)
            for j, offset in enumerate((-3, -2, 2, 3)):
                at = jnp.clip(number + offset, 0, 2**t - 1)
                block = lower if offset < 0 else upper
                block = jnp.where(lax.rem(at, 2) == j % 2, block, swap(block))
                kept = jnp.where(lefts == (lax.rem(at, 2) == 0), block, 0.0)
                abuf[offsets[t] + at // 2] = abuf[offsets[t] + at // 2] + kept

        abuf[0:2] = jnp.zeros((2, 64, 128), F32)
        for t in range(2, 6):
            pltpu.make_async_copy(dbuf.at[t - 2], dbuf.at[t - 2], d_recv.at[t - 2]).wait()
            add(t, mm(chain[t], dbuf[t - 2, 0], NN), mm(chain[t], dbuf[t - 2, 1], NN))

            def widen(i, carry):
                tile = abuf[offsets[t] + i]
                for half in range(2):
                    x = tile[:, 0:64] if half == 0 else swap(tile)[:, 0:64]
                    n = 2 * i + half
                    e = ut[pl.ds(2 ** (t + 1) - 2 + 2 * n, 2)].reshape(128, 64)
                    abuf[offsets[t + 1] + n] = mm(x, e, NT)
                return carry

            lax.fori_loop(0, 2 ** (t - 1), widen, 0, unroll=2)
        add(6, *by_offset(k6, [middle_lists[0, k] for k in range(4)], g))

        def keep(i, carry):
            high, low = parts(abuf[30 + i])
            ahigh[i] = high
            alow[i] = low
            return carry

        lax.fori_loop(0, 32, keep, 0, unroll=4)
        root = jnp.zeros((8, 64), F32)
        return mm(root, chain[0], NT)

    def upper(p):
        for c in ags[p]:
            c.wait_recv()
        sent.extend(ags[p])
        total = None
        for x in range(2):
            for z in range(8):
                zslot = lax.rem(gz - z + 8, 8)
                even = agbuf[p, zslot, gc, x]
                odd = agbuf[p, zslot, 1 - gc, x]
                for h in range(2):
                    both = jnp.where(left, even, swap(odd)) if h == 0 else jnp.where(left, swap(even), odd)
                    i = (2 * x + h) * 8 + z
                    xs = stacked(both)
                    term = dot(xs, ahigh[i], NT) + dot(xs, alow[i], NT)
                    total = term if total is None else total + term
        return total[:8] + total[8:]

    def finish(p, base, w6):
        w10 = base + mm(w6, q6s[...], NT)
        spread = jnp.concatenate([jnp.where(quarter == l, w10, 0.0) for l in range(4)], axis=0)
        rows = mm(spread, basis[...].reshape(256, 256), NN) + acc[...]
        for l in range(4):
            outs[p, l] = rows[8 * l : 8 * l + 8]
        return rows

    rows = jnp.concatenate([vlf[4 + 4 * q + l] for l in range(4)], axis=0)
    climb(0, rows)

    @pl.when(q == 0)
    def _():
        for k in range(4):
            view = vin.at[2 * k : 2 * k + 2, 0:8]
            pltpu.make_async_copy(view, view, edge_recv.at[0, k]).wait()
        for i in range(4):
            vlf[i] = vin[:, 4 + i, :]

    @pl.when(q == 3)
    def _():
        for k in range(4):
            view = vin.at[2 * k : 2 * k + 2, 24:32]
            pltpu.make_async_copy(view, view, edge_recv.at[1, k]).wait()
        for i in range(4):
            vlf[20 + i] = vin[:, 24 + i, :]

    ld_near.wait()
    near_field(vlf, 16 * g - 4, 4 * q)
    middle(0)
    for c in ld_k[:4]:
        c.wait()
    root_part = upper_operator()
    base = local_coupled(0) + middle_coupled(0)
    first = finish(0, base, upper(0) + root_part)
    for l in range(4):
        vnext[4 + l] = first[8 * l : 8 * l + 8]
    vs = [
        remote(vnext.at[4:8], vnext.at[0:4], v_send.at[0], v_recv.at[0], linear(1)),
        remote(vnext.at[4:8], vnext.at[8:12], v_send.at[1], v_recv.at[1], linear(-1)),
    ]
    out0 = pltpu.make_async_copy(outs.at[0], first_hbm, out_sem.at[0])
    out0.start()

    climb(1, first)
    for c in vs:
        c.wait_recv()
    sent.extend(vs)
    near_field(vnext, 4 * d - 4, 0)
    middle(1)
    base = local_coupled(1) + middle_coupled(1)
    finish(1, base, upper(1) + root_part)
    out1 = pltpu.make_async_copy(outs.at[1], second_hbm, out_sem.at[1])
    out1.start()

    for c in sent:
        c.wait_send()

    def given(i, carry):
        @pl.when(first_below + i != g)
        def _():
            pltpu.make_async_copy(dsend, dsend, d_send.at[i]).wait()

        return carry

    lax.fori_loop(0, count, given, 0)
    out0.wait()
    out1.wait()


def body(
    input_columns,
    near_blocks,
    near_pairs,
    leaf_basis,
    local_transfer,
    local_coupling,
    local_lists,
    middle_transfer,
    middle_coupling,
    middle_lists,
    upper_transfer,
    upper_coupling,
    upper_lists,
):
    smem = pl.BlockSpec(memory_space=pltpu.SMEM)
    anywhere = pl.BlockSpec(memory_space=pl.ANY)
    vm = lambda *shape: pltpu.VMEM(shape, F32)
    dma = lambda *shape: pltpu.SemaphoreType.DMA(shape)
    first, second = pl.pallas_call(
        kernel,
        out_shape=[jax.ShapeDtypeStruct((4, 8, 256), F32)] * 2,
        in_specs=[smem] * 4 + [anywhere] * 9,
        out_specs=[anywhere] * 2,
        scratch_shapes=[
            vm(8, 32, 256), vm(24, 8, 256), vm(12, 8, 256), vm(32, 256, 256), vm(4, 64, 256),
            vm(4, 64, 64), vm(2, 64, 64), vm(64, 64), vm(64, 64),
            vm(4, 4, 64, 64), vm(2, 4, 64, 64), vm(4, 64, 64), vm(4, 64, 64), vm(4, 64, 64),
            vm(126, 64, 64), vm(4, 64, 64),
            vm(2, 64, 128), vm(4, 2, 64, 128), vm(62, 64, 128),
            pltpu.VMEM((32, 64, 128), BF16), pltpu.VMEM((32, 64, 128), BF16),
            vm(256, 256), vm(256, 64), vm(256, 64), vm(256, 64),
            vm(7, 4, 8, 128), vm(7, 4, 8, 128), vm(2, 4, 4, 8, 128), vm(2, 2, 8, 128), vm(2, 8, 2, 2, 8, 128),
            vm(5, 8, 128), vm(5, 8, 128), vm(32, 256), vm(2, 4, 8, 256),
            dma(16), dma(4), dma(4), dma(2), dma(2, 4), dma(16), dma(4),
            dma(2, 4, 4), dma(2, 4, 4), dma(2, 7), dma(2, 7), dma(2, 8, 2), dma(2, 8, 2),
            dma(2, 5), dma(2, 5), dma(2), dma(2), dma(2),
        ],
        compiler_params=pltpu.CompilerParams(
            collective_id=0, has_side_effects=True, vmem_limit_bytes=48 * 2**20
        ),
    )(
        near_pairs.T, local_lists.T, middle_lists, upper_lists,
        input_columns, near_blocks, leaf_basis, local_transfer, local_coupling,
        middle_transfer, middle_coupling, upper_transfer, upper_coupling,
    )
    return (first.transpose(1, 0, 2), second.transpose(1, 0, 2))


def solution(mesh):
    in_specs = (
        P("rhs", "leaf", None),
        P(("leaf", "rhs"), None, None),
        P(("leaf", "rhs"), None),
        P(("leaf", "rhs"), None, None),
        P("leaf", None, None),
        P("leaf", None, None, None),
        P("leaf", None),
        P("leaf", None, None),
        P("leaf", None, None, None),
        P("leaf", None),
        P(),
        P("leaf", None, None, None),
        P("leaf", None),
    )
    out_specs = (P(None, ("leaf", "rhs"), None), P(None, ("leaf", "rhs"), None))
    return jax.shard_map(body, mesh=mesh, in_specs=in_specs, out_specs=out_specs, check_vma=False)
```

```python
import jax
import jax.numpy as jnp
from jax import lax
from jax.experimental import pallas as pl
from jax.experimental.pallas import tpu as pltpu
from jax.sharding import PartitionSpec as P

F32 = jnp.float32
BF16 = jnp.bfloat16
MESH = pl.DeviceIdType.MESH
NN = (((1,), (0,)), ((), ()))
NT = (((1,), (1,)), ((), ()))
XY = [(i, k) for i in range(4) for k in range(4) if (i, k) != (0, 0)]
XY_ORDER = sorted(XY, key=lambda s: -(min(s[0], 4 - s[0]) + min(s[1], 4 - s[1])))
ZC_ORDER = [(4, 0), (4, 1), (3, 0), (3, 1), (5, 0), (5, 1), (2, 0), (2, 1), (6, 0), (6, 1), (1, 0), (1, 1), (7, 0), (7, 1), (0, 1)]
ZC_NEAR = [(2, 0), (2, 1), (6, 0), (6, 1), (1, 0), (1, 1), (7, 0), (7, 1), (0, 1)]


def stacked(x):
    high = x.astype(BF16).astype(F32)
    return jnp.concatenate([high, x - high], axis=0).astype(BF16)


def parts(w):
    high = w.astype(BF16)
    return high, (w - high.astype(F32)).astype(BF16)


def dot(x, w, dims):
    return lax.dot_general(x, w, dims, preferred_element_type=F32)


def mm_parts(xs, high, low, dims):
    y = dot(xs, high, dims) + dot(xs, low, dims)
    rows = xs.shape[0] // 2
    return y[:rows] + y[rows:]


def mm(x, w, dims):
    return mm_parts(stacked(x), *parts(w), dims)


def left_lanes(shape):
    return lax.broadcasted_iota(jnp.int32, shape, len(shape) - 1) < 64


def swap(x):
    return pltpu.roll(x, 64, x.ndim - 1)


def kernel(
    pairs, local_lists, middle_lists, upper_lists,
    columns, near_hbm, basis_hbm, lt_hbm, lc_hbm, mt_hbm, mc_hbm, ut_hbm, uc_hbm,
    first_hbm, second_hbm,
    vin, vlf, vnext, near, basis, e10, e9, e8, e7, k10, k9, k8, k7, k6, utt, ut, uc,
    dsend, dbuf, u_high, u_low, v_high, v_low, gmap, ctile, wup, q6s, q7s, q8s,
    halo_0, halo_1, xybuf, agsend, agbuf, c7_0, c7_1, acc, outs,
    load_sem, in_send, in_recv, edge_send, edge_recv, d_send, d_recv,
    xy_send, xy_recv, halo_send, halo_recv, ag_send, ag_recv, c7_send, c7_recv, v_send, v_recv, out_sem,
    ready_xy, ready_z, ready_group, ready_plane,
):
    halo, c7buf = (halo_0, halo_1), (c7_0, c7_1)
    g = lax.axis_index("leaf")
    q = lax.axis_index("rhs")
    d = 4 * g + q
    gx = g // 16
    zc = lax.rem(g, 16)
    gz, gc = zc // 2, lax.rem(zc, 2)

    def linear(k):
        e = lax.rem(d + k + 256, 256)
        return (e // 4, lax.rem(e, 4))

    def group(k):
        return lax.rem(g + k + 64, 64)

    def xy(i, k):
        return (lax.rem(gx + i, 4) * 16 + zc, lax.rem(q + k, 4))

    def zcs(i, k):
        return (gx * 16 + lax.rem(gz + i, 8) * 2 + lax.rem(gc + k, 2), q)

    loads = []

    def load(src, dst):
        c = pltpu.make_async_copy(src, dst, load_sem.at[len(loads)])
        c.start()
        loads.append(c)
        return c

    ld_own = load(columns, vin.at[pl.ds(2 * q, 2), 8:24])
    ld_ut = load(ut_hbm, utt)
    ld_e = [
        load(lt_hbm.at[pl.ds(12 + 4 * q, 4)], e10),
        load(lt_hbm.at[pl.ds(4 + 2 * q, 2)], e9),
        load(lt_hbm.at[q], e8),
        load(mt_hbm.at[q // 2], e7),
    ]
    ld_basis = load(basis_hbm, basis)
    ld_uc = load(uc_hbm.at[0], uc)
    ld_k = [
        load(lc_hbm.at[pl.ds(12 + 4 * q, 4)], k10),
        load(lc_hbm.at[pl.ds(4 + 2 * q, 2)], k9),
        load(lc_hbm.at[q], k8),
        load(mc_hbm.at[1 + q // 2], k7),
        load(mc_hbm.at[0], k6),
    ]
    ld_near = load(near_hbm, near)

    level = 2 + (g >= 8).astype(jnp.int32) + (g >= 16).astype(jnp.int32) + (g >= 32).astype(jnp.int32)
    count = jnp.where(g >= 32, 2, jnp.where(g >= 16, 4, jnp.where(g >= 8, 8, jnp.where(g >= 4, 16, 0))))
    start = jnp.where(g >= 32, 32, jnp.where(g >= 16, 16, jnp.where(g >= 8, 8, 4)))
    own_number = g - start
    first_below = own_number * count
    own_inside = jnp.where((g >= first_below) & (g < first_below + count), 1, 0)
    barrier = pltpu.get_barrier_semaphore()

    def greet(device):
        pl.semaphore_signal(barrier, inc=1, device_id=device, device_id_type=MESH)

    for k in (1, 2, 3):
        greet(xy(0, k))
        greet(xy(k, 0))
    for z in ZC_NEAR:
        greet(zcs(*z))
    for k in (4, -4, 8, -8):
        greet(linear(k))
    ld_ut.wait()
    for a in range(64):
        ut[pl.ds(a, 126, stride=64), :] = utt[a].T
    pl.semaphore_wait(barrier, 6 + len(ZC_NEAR) + 4)

    def tell(semaphore, device):
        pl.semaphore_signal(semaphore, inc=1, device_id=device, device_id_type=MESH)

    def remote(src, dst, ss, rs, device):
        c = pltpu.make_async_remote_copy(
            src_ref=src, dst_ref=dst, send_sem=ss, recv_sem=rs, device_id=device, device_id_type=MESH
        )
        c.start()
        return c

    sent = []
    ins = []
    for k in (2, 1, 3):
        ins.append(
            remote(columns, vin.at[pl.ds(2 * q, 2), 8:24], in_send.at[k], in_recv.at[k], (g, lax.rem(q + k, 4)))
        )
    for k in (1, 2, 3):
        tell(ready_xy, xy(k, 0))
    for k in (2, 6):
        tell(ready_z, zcs(k, 0))
    for k in (1, -1):
        tell(ready_group, (group(k), q))

    def by_offset(blocks, entries, number):
        found = []
        for offset in (-3, -2, 2, 3):
            total = None
            for k in range(4):
                weight = jnp.where((entries[k] >= 0) & (entries[k] == number + offset), 1.0, 0.0)
                term = blocks[k] * weight
                total = term if total is None else total + term
            found.append(total)
        return (jnp.concatenate(found[:2], axis=1), jnp.concatenate(found[2:], axis=1))

    ld_uc.wait()
    low_half, high_half = by_offset(uc, [upper_lists[0, k] for k in range(4)], own_number)
    dsend[0] = low_half
    dsend[1] = high_half

    def matrix(n, many=1):
        return ut[pl.ds(pl.multiple_of(64 * n, 64), 64 * many), :]

    def pair(t, n):
        return matrix(2**t - 2 + 2 * n, 2)

    for n in range(16):
        for m in range(2):
            high, low = parts(mm(pair(6, 2 * n + m), matrix(2**5 - 2 + 2 * n + m), NN))
            u_high[n, 128 * m : 128 * m + 128] = high
            u_low[n, 128 * m : 128 * m + 128] = low
    for n in range(4):
        for m in range(2):
            high, low = parts(mm(pair(4, 2 * n + m), matrix(2**3 - 2 + 2 * n + m), NN))
            v_high[n, 128 * m : 128 * m + 128] = high
            v_low[n, 128 * m : 128 * m + 128] = low
    chain = {5: matrix(2**6 - 2 + g)}
    for t in (4, 3, 2, 1, 0):
        chain[t] = mm(chain[t + 1], matrix(2 ** (t + 1) - 2 + g // 2 ** (5 - t)), NN)
    root_part = mm(jnp.zeros((8, 64), F32), chain[0], NT)
    for t in range(2, 6):
        gmap[t - 2, 2] = jnp.concatenate([chain[t], chain[t]], axis=1)
    pl.semaphore_wait(ready_z, 2)
    for k in (1, 2, 3):
        tell(ready_plane, xy(k, 0))

    for c in ld_e:
        c.wait()
    q8 = jnp.concatenate([mm(e10[l], e9[l // 2], NN) for l in range(4)], axis=0)
    q7 = mm(q8, e8[...], NN)
    q6 = mm(q7, e7[...], NN)
    q8s[...] = q8
    q7s[...] = q7
    q6s[...] = q6
    wup[:, 0:128] = jnp.concatenate([q7, q6], axis=1)
    wup[:, 128:256] = jnp.concatenate([q8, q8], axis=1)

    left = left_lanes((8, 128))
    quarter = lax.broadcasted_iota(jnp.int32, (8, 256), 1) // 64
    ld_own.wait()
    ld_basis.wait()
    for c in ins:
        c.wait_recv()
    sent.extend(ins)
    for i in range(16):
        vlf[4 + i] = vin[:, 8 + i, :]

    def climb(p, rows):
        wide = mm(rows, basis[...].reshape(256, 256), NT)
        c10 = jnp.zeros((8, 256), F32)
        for l in range(4):
            c10 = jnp.where(quarter == l, wide[8 * l : 8 * l + 8], c10)
        tops = mm(c10, wup[...], NN)
        xybuf[p, 0, 0] = tops[:, 0:128]
        halo[p][3, 3] = tops[:, 128:256]
        for i, k in XY_ORDER:
            xys[p].append(
                remote(xybuf.at[p, 0, 0], xybuf.at[p, i, k], xy_send.at[p, i, k], xy_recv.at[p, i, k], xy(i, k))
            )
        halo[p][3, 0] = c10[:, 0:128]
        halo[p][3, 1] = c10[:, 128:256]
        halo[p][3, 2] = jnp.concatenate(
            [mm(c10[:, 128 * j : 128 * j + 128], e10[2 * j : 2 * j + 2].reshape(128, 64), NN) for j in range(2)], axis=1
        )
        for k in (1, -1, 2, -2, 3, -3):
            tiles = pl.ds({1: 0, 2: 2, 3: 3}[abs(k)], {1: 4, 2: 2, 3: 1}[abs(k)])
            halos[p].append(
                remote(
                    halo[p].at[3, tiles], halo[p].at[3 - k, tiles], halo_send.at[p, 3 - k], halo_recv.at[p, 3 - k], linear(k)
                )
            )

    xys, halos, ags, c7s = ([], []), ([], []), ([], []), ([], [])

    def near_field(vectors, offset, least):
        def step(s, totals):
            target = pairs[0, s] - 4 * d
            source = jnp.clip(pairs[1, s] - offset, least, least + 11)
            term = mm(vectors[source], near[s], NT)
            return tuple(t + term * jnp.where(target == l, 1.0, 0.0) for l, t in enumerate(totals))

        zero = jnp.zeros((8, 256), F32)
        totals = lax.fori_loop(0, 32, step, (zero,) * 4, unroll=4)
        for l in range(4):
            acc[8 * l : 8 * l + 8] = totals[l]

    def half_of(tile, half):
        return jnp.where(half == 1, swap(tile), tile)[:, 0:64]

    def coupled(blocks, entries, pick):
        total = None
        for k in range(4):
            x = pick(entries[k]) * jnp.where(entries[k] >= 0, 1.0, 0.0)
            term = mm(x, blocks[k], NT)
            total = term if total is None else total + term
        return total

    def local_coupled(p):
        for c in halos[p]:
            c.wait_recv()
        sent.extend(halos[p])

        def pick10(entry):
            at = jnp.clip(entry - 4 * d + 12, 0, 27)
            return half_of(halo[p][at // 4, lax.rem(at, 4) // 2], lax.rem(at, 2))

        def pick9(entry):
            at = jnp.clip(entry - 2 * d + 6, 0, 13)
            return half_of(halo[p][at // 2, 2], lax.rem(at, 2))

        def pick8(entry):
            at = jnp.clip(entry - d + 3, 0, 6)
            return halo[p][at, 3][:, 0:64]

        z10 = [coupled(k10[l], [local_lists[k, 12 + 4 * q + l] for k in range(4)], pick10) for l in range(4)]
        z9 = [coupled(k9[j], [local_lists[k, 4 + 2 * q + j] for k in range(4)], pick9) for j in range(2)]
        z8 = coupled(k8, [local_lists[k, q] for k in range(4)], pick8)
        down = mm(z8, q8s[...], NT)
        below = [mm(z9[j], e10[2 * j : 2 * j + 2].reshape(128, 64), NT) for j in range(2)]
        return down + jnp.concatenate(
            [below[0] + jnp.concatenate(z10[0:2], axis=1), below[1] + jnp.concatenate(z10[2:4], axis=1)], axis=1
        )

    def middle(p):
        for c in xys[p]:
            c.wait_recv()
        sent.extend(xys[p])
        totals = []
        for x in range(4):
            i = lax.rem(gx - x + 4, 4)
            totals.append(xybuf[p, i, 0] + xybuf[p, i, 1] + xybuf[p, i, 2] + xybuf[p, i, 3])
        for j in range(2):
            agsend[p, j] = jnp.where(left, swap(totals[2 * j]), totals[2 * j + 1])
        for i, k in ZC_ORDER:
            ags[p].append(
                remote(agsend.at[p], agbuf.at[p, i, k], ag_send.at[p, i, k], ag_recv.at[p, i, k], zcs(i, k))
            )
        agbuf[p, 0, 0] = agsend[p]

        def own(y):
            return xybuf[p, 0, lax.rem(q - y + 4, 4)]

        c7buf[p][2] = jnp.where(left, own(0) + own(1), swap(own(2) + own(3)))
        for k in (1, -1, 2, -2):
            c7s[p].append(
                remote(c7buf[p].at[2], c7buf[p].at[2 - k], c7_send.at[p, 2 - k], c7_recv.at[p, 2 - k], (group(k), q))
            )

    def middle_coupled(p):
        for c in c7s[p]:
            c.wait_recv()
        sent.extend(c7s[p])

        def pick7(entry):
            at = jnp.clip(entry - 2 * g + 4, 0, 9)
            return half_of(c7buf[p][at // 2], lax.rem(at, 2))

        z7 = coupled(k7, [middle_lists[1 + q // 2, k] for k in range(4)], pick7)
        return mm(z7, q7s[...], NT)

    def upper_maps():
        for t in range(2, 6):
            pltpu.make_async_copy(dbuf.at[t - 2], dbuf.at[t - 2], d_recv.at[t - 2]).wait()
            down = gmap[t - 2, 2][:, 0:64]
            for half in range(2):
                gmap[t - 2, half] = mm(down, dbuf[t - 2, half], NN)
        ld_k[4].wait()
        lower, upper = by_offset(k6, [middle_lists[0, k] for k in range(4)], g)
        gmap[4, 0] = lower
        gmap[4, 1] = upper

    def upper(p):
        for c in ags[p]:
            c.wait_recv()
        sent.extend(ags[p])
        roots = []
        for x in range(2):
            line = []
            for z in range(8):
                zslot = lax.rem(gz - z + 8, 8)
                even = agbuf[p, zslot, gc, x]
                odd = agbuf[p, zslot, 1 - gc, x]
                line.append((jnp.where(left, even, swap(odd)), jnp.where(left, swap(even), odd)))
            roots.extend([a for a, b in line] + [b for a, b in line])
        for i in range(32):
            ctile[16 + i] = roots[i]
        quads = []
        for n in range(16):
            x = jnp.concatenate([roots[2 * n], roots[2 * n + 1]], axis=1)
            quads.append(mm_parts(stacked(x), u_high[n], u_low[n], NN))
        fours = [jnp.concatenate([quads[2 * n], quads[2 * n + 1]], axis=1) for n in range(8)]
        for n in range(8):
            ctile[n] = fours[n]
        total = root_part
        for t in range(2, 7):
            number = g // 2 ** (6 - t)
            for half, offsets in enumerate(((-3, -2), (2, 3))):
                found = []
                for offset in offsets:
                    n = jnp.clip(number + offset, 0, 2**t - 1)
                    if t == 6:
                        c = half_of(ctile[16 + n // 2], lax.rem(n, 2))
                    elif t == 5:
                        c = mm(ctile[16 + n], pair(6, n), NN)
                    elif t == 4:
                        c = half_of(ctile[n // 2], lax.rem(n, 2))
                    elif t == 3:
                        c = mm(ctile[n], pair(4, n), NN)
                    else:
                        x = jnp.concatenate([ctile[2 * n], ctile[2 * n + 1]], axis=1)
                        c = mm_parts(stacked(x), v_high[n], v_low[n], NN)
                    found.append(c)
                total = total + mm(jnp.concatenate(found, axis=1), gmap[t - 2, half], NT)
        return total

    def finish(p, base, w6):
        w10 = base + mm(w6, q6s[...], NT)
        spread = jnp.concatenate([jnp.where(quarter == l, w10, 0.0) for l in range(4)], axis=0)
        rows = mm(spread, basis[...].reshape(256, 256), NN) + acc[...]
        for l in range(4):
            outs[p, l] = rows[8 * l : 8 * l + 8]
        return rows

    rows = jnp.concatenate([vlf[4 + 4 * q + l] for l in range(4)], axis=0)
    pl.semaphore_wait(ready_xy, 3)
    pl.semaphore_wait(ready_group, 2)
    climb(0, rows)
    sent.append(remote(columns.at[:, 8:16], vin.at[pl.ds(2 * q, 2), 0:8], edge_send.at[0], edge_recv.at[0, q], (group(1), 0)))
    sent.append(remote(columns.at[:, 0:8], vin.at[pl.ds(2 * q, 2), 24:32], edge_send.at[1], edge_recv.at[1, q], (group(-1), 3)))
    pl.semaphore_wait(ready_plane, 3)

    def give(i, carry):
        to = first_below + i

        @pl.when(to != g)
        def _():
            remote(dsend, dbuf.at[level - 2], d_send.at[i], d_recv.at[level - 2], (to, q))

        @pl.when(to == g)
        def _():
            pltpu.make_async_copy(dsend, dbuf.at[level - 2], d_recv.at[level - 2]).start()

        return carry

    lax.fori_loop(0, count, give, 0)


    @pl.when(q == 0)
    def _():
        for k in range(4):
            view = vin.at[2 * k : 2 * k + 2, 0:8]
            pltpu.make_async_copy(view, view, edge_recv.at[0, k]).wait()
        for i in range(4):
            vlf[i] = vin[:, 4 + i, :]

    @pl.when(q == 3)
    def _():
        for k in range(4):
            view = vin.at[2 * k : 2 * k + 2, 24:32]
            pltpu.make_async_copy(view, view, edge_recv.at[1, k]).wait()
        for i in range(4):
            vlf[20 + i] = vin[:, 24 + i, :]

    ld_near.wait()
    near_field(vlf, 16 * g - 4, 4 * q)
    middle(0)
    for c in ld_k[:4]:
        c.wait()
    upper_maps()
    base = local_coupled(0) + middle_coupled(0)
    first = finish(0, base, upper(0))
    for l in range(4):
        vnext[4 + l] = first[8 * l : 8 * l + 8]
    vs = [
        remote(vnext.at[4:8], vnext.at[0:4], v_send.at[0], v_recv.at[0], linear(1)),
        remote(vnext.at[4:8], vnext.at[8:12], v_send.at[1], v_recv.at[1], linear(-1)),
    ]
    out0 = pltpu.make_async_copy(outs.at[0], first_hbm, out_sem.at[0])
    out0.start()

    climb(1, first)
    for c in vs:
        c.wait_recv()
    sent.extend(vs)
    near_field(vnext, 4 * d - 4, 0)
    middle(1)
    base = local_coupled(1) + middle_coupled(1)
    finish(1, base, upper(1))
    out1 = pltpu.make_async_copy(outs.at[1], second_hbm, out_sem.at[1])
    out1.start()

    for c in sent:
        c.wait_send()

    def given(i, carry):
        @pl.when(first_below + i != g)
        def _():
            pltpu.make_async_copy(dsend, dsend, d_send.at[i]).wait()

        return carry

    lax.fori_loop(0, count, given, 0)
    out0.wait()
    out1.wait()


def body(
    input_columns,
    near_blocks,
    near_pairs,
    leaf_basis,
    local_transfer,
    local_coupling,
    local_lists,
    middle_transfer,
    middle_coupling,
    middle_lists,
    upper_transfer,
    upper_coupling,
    upper_lists,
):
    smem = pl.BlockSpec(memory_space=pltpu.SMEM)
    anywhere = pl.BlockSpec(memory_space=pl.ANY)
    vm = lambda *shape: pltpu.VMEM(shape, F32)
    dma = lambda *shape: pltpu.SemaphoreType.DMA(shape)
    first, second = pl.pallas_call(
        kernel,
        out_shape=[jax.ShapeDtypeStruct((4, 8, 256), F32)] * 2,
        in_specs=[smem] * 4 + [anywhere] * 9,
        out_specs=[anywhere] * 2,
        scratch_shapes=[
            vm(8, 32, 256), vm(24, 8, 256), vm(12, 8, 256), vm(32, 256, 256), vm(4, 64, 256),
            vm(4, 64, 64), vm(2, 64, 64), vm(64, 64), vm(64, 64),
            vm(4, 4, 64, 64), vm(2, 4, 64, 64), vm(4, 64, 64), vm(4, 64, 64), vm(4, 64, 64),
            vm(64, 64, 126), vm(126 * 64, 64), vm(4, 64, 64),
            vm(2, 64, 128), vm(4, 2, 64, 128),
            pltpu.VMEM((16, 256, 64), BF16), pltpu.VMEM((16, 256, 64), BF16),
            pltpu.VMEM((4, 256, 64), BF16), pltpu.VMEM((4, 256, 64), BF16),
            vm(5, 3, 64, 128), vm(48, 8, 128),
            vm(256, 256), vm(256, 64), vm(256, 64), vm(256, 64),
            vm(7, 4, 8, 128), vm(7, 4, 8, 128), vm(2, 4, 4, 8, 128), vm(2, 2, 8, 128), vm(2, 8, 2, 2, 8, 128),
            vm(5, 8, 128), vm(5, 8, 128), vm(32, 256), vm(2, 4, 8, 256),
            dma(16), dma(4), dma(4), dma(2), dma(2, 4), dma(16), dma(4),
            dma(2, 4, 4), dma(2, 4, 4), dma(2, 7), dma(2, 7), dma(2, 8, 2), dma(2, 8, 2),
            dma(2, 5), dma(2, 5), dma(2), dma(2), dma(2),
            *[pltpu.SemaphoreType.REGULAR] * 4,
        ],
        compiler_params=pltpu.CompilerParams(
            collective_id=0, has_side_effects=True, vmem_limit_bytes=62 * 2**20
        ),
    )(
        near_pairs.T, local_lists.T, middle_lists, upper_lists,
        input_columns, near_blocks, leaf_basis, local_transfer, local_coupling,
        middle_transfer, middle_coupling, upper_transfer.transpose(1, 2, 0), upper_coupling,
    )
    return (first.transpose(1, 0, 2), second.transpose(1, 0, 2))


def solution(mesh):
    in_specs = (
        P("rhs", "leaf", None),
        P(("leaf", "rhs"), None, None),
        P(("leaf", "rhs"), None),
        P(("leaf", "rhs"), None, None),
        P("leaf", None, None),
        P("leaf", None, None, None),
        P("leaf", None),
        P("leaf", None, None),
        P("leaf", None, None, None),
        P("leaf", None),
        P(),
        P("leaf", None, None, None),
        P("leaf", None),
    )
    out_specs = (P(None, ("leaf", "rhs"), None), P(None, ("leaf", "rhs"), None))
    return jax.shard_map(body, mesh=mesh, in_specs=in_specs, out_specs=out_specs, check_vma=False)
```

```python
import jax
import jax.numpy as jnp
from jax import lax
from jax.experimental import pallas as pl
from jax.experimental.pallas import tpu as pltpu
from jax.sharding import PartitionSpec as P

F32 = jnp.float32
BF16 = jnp.bfloat16
MESH = pl.DeviceIdType.MESH
NN = (((1,), (0,)), ((), ()))
NT = (((1,), (1,)), ((), ()))
XY = [(i, k) for i in range(4) for k in range(4) if (i, k) != (0, 0)]
XY_ORDER = sorted(XY, key=lambda s: -(min(s[0], 4 - s[0]) + min(s[1], 4 - s[1])))
ZC_ORDER = [(4, 0), (4, 1), (3, 0), (3, 1), (5, 0), (5, 1), (2, 0), (2, 1), (6, 0), (6, 1), (1, 0), (1, 1), (7, 0), (7, 1), (0, 1)]
ZC_NEAR = [(2, 0), (2, 1), (6, 0), (6, 1), (1, 0), (1, 1), (7, 0), (7, 1), (0, 1)]


def stacked(x):
    high = x.astype(BF16).astype(F32)
    return jnp.concatenate([high, x - high], axis=0).astype(BF16)


def parts(w):
    high = w.astype(BF16)
    return high, (w - high.astype(F32)).astype(BF16)


def dot(x, w, dims):
    return lax.dot_general(x, w, dims, preferred_element_type=F32)


def mm_parts(xs, high, low, dims):
    y = dot(xs, high, dims) + dot(xs, low, dims)
    rows = xs.shape[0] // 2
    return y[:rows] + y[rows:]


def mm(x, w, dims):
    return mm_parts(stacked(x), *parts(w), dims)


def left_lanes(shape):
    return lax.broadcasted_iota(jnp.int32, shape, len(shape) - 1) < 64


def swap(x):
    return pltpu.roll(x, 64, x.ndim - 1)


def kernel(
    pairs, local_lists, middle_lists, upper_lists,
    columns, near_hbm, basis_hbm, lt_hbm, lc_hbm, mt_hbm, mc_hbm, ut_hbm, uc_hbm,
    first_hbm, second_hbm,
    vin, vlf, vnext, near, basis, e10, e9, e8, e7, k10, k9, k8, k7, k6, utt, ut, uc,
    dsend, dbuf, u_high, u_low, v_high, v_low, gmap, ctile, wup, q6s, q7s, q8s,
    halo_0, halo_1, xybuf, agsend, agbuf, c7_0, c7_1, acc, outs,
    load_sem, in_send, in_recv, edge_send, edge_recv, d_send, d_recv,
    xy_send, xy_recv, halo_send, halo_recv, ag_send, ag_recv, c7_send, c7_recv, v_send, v_recv, out_sem,
    share_send, share_recv, ready_xy, ready_z, ready_group, ready_plane,
):
    halo, c7buf = (halo_0, halo_1), (c7_0, c7_1)
    g = lax.axis_index("leaf")
    q = lax.axis_index("rhs")
    d = 4 * g + q
    gx = g // 16
    zc = lax.rem(g, 16)
    gz, gc = zc // 2, lax.rem(zc, 2)

    def linear(k):
        e = lax.rem(d + k + 256, 256)
        return (e // 4, lax.rem(e, 4))

    def group(k):
        return lax.rem(g + k + 64, 64)

    def xy(i, k):
        return (lax.rem(gx + i, 4) * 16 + zc, lax.rem(q + k, 4))

    def zcs(i, k):
        return (gx * 16 + lax.rem(gz + i, 8) * 2 + lax.rem(gc + k, 2), q)

    loads = []

    def load(src, dst):
        c = pltpu.make_async_copy(src, dst, load_sem.at[len(loads)])
        c.start()
        loads.append(c)
        return c

    ld_own = load(columns, vin.at[pl.ds(2 * q, 2), 8:24])
    ld_ut = load(ut_hbm, utt)
    ld_e = [
        load(lt_hbm.at[pl.ds(12 + 4 * q, 4)], e10),
        load(lt_hbm.at[pl.ds(4 + 2 * q, 2)], e9),
        load(lt_hbm.at[q], e8),
        load(mt_hbm.at[q // 2], e7),
    ]
    ld_basis = load(basis_hbm, basis)
    ld_uc = load(uc_hbm.at[0], uc)
    ld_k = [
        load(lc_hbm.at[pl.ds(12 + 4 * q, 4)], k10),
        load(lc_hbm.at[pl.ds(4 + 2 * q, 2)], k9),
        load(lc_hbm.at[q], k8),
        load(mc_hbm.at[1 + q // 2], k7),
        load(mc_hbm.at[0], k6),
    ]
    ld_near = load(near_hbm, near)

    level = 2 + (g >= 8).astype(jnp.int32) + (g >= 16).astype(jnp.int32) + (g >= 32).astype(jnp.int32)
    count = jnp.where(g >= 32, 2, jnp.where(g >= 16, 4, jnp.where(g >= 8, 8, jnp.where(g >= 4, 16, 0))))
    start = jnp.where(g >= 32, 32, jnp.where(g >= 16, 16, jnp.where(g >= 8, 8, 4)))
    own_number = g - start
    first_below = own_number * count
    own_inside = jnp.where((g >= first_below) & (g < first_below + count), 1, 0)
    barrier = pltpu.get_barrier_semaphore()

    def greet(device):
        pl.semaphore_signal(barrier, inc=1, device_id=device, device_id_type=MESH)

    for k in (1, 2, 3):
        greet(xy(0, k))
        greet(xy(k, 0))
    for z in ZC_NEAR:
        greet(zcs(*z))
    for k in (4, -4, 8, -8):
        greet(linear(k))
    ld_ut.wait()
    for a in range(64):
        ut[pl.ds(a, 126, stride=64), :] = utt[a].T
    pl.semaphore_wait(barrier, 6 + len(ZC_NEAR) + 4)

    def tell(semaphore, device):
        pl.semaphore_signal(semaphore, inc=1, device_id=device, device_id_type=MESH)

    def remote(src, dst, ss, rs, device):
        c = pltpu.make_async_remote_copy(
            src_ref=src, dst_ref=dst, send_sem=ss, recv_sem=rs, device_id=device, device_id_type=MESH
        )
        c.start()
        return c

    sent = []
    ins = []
    for k in (2, 1, 3):
        ins.append(
            remote(columns, vin.at[pl.ds(2 * q, 2), 8:24], in_send.at[k], in_recv.at[k], (g, lax.rem(q + k, 4)))
        )
    for k in (1, 2, 3):
        tell(ready_xy, xy(k, 0))
    for k in (2, 6):
        tell(ready_z, zcs(k, 0))
    for k in (1, -1):
        tell(ready_group, (group(k), q))

    def by_offset(blocks, entries, number):
        found = []
        for offset in (-3, -2, 2, 3):
            total = None
            for k in range(4):
                weight = jnp.where((entries[k] >= 0) & (entries[k] == number + offset), 1.0, 0.0)
                term = blocks[k] * weight
                total = term if total is None else total + term
            found.append(total)
        return (jnp.concatenate(found[:2], axis=1), jnp.concatenate(found[2:], axis=1))

    ld_uc.wait()
    quarter_rows = pl.ds(pl.multiple_of(16 * q, 16), 16)
    low_half, high_half = by_offset(
        [uc[k, quarter_rows, :] for k in range(4)], [upper_lists[0, k] for k in range(4)], own_number
    )
    dsend[0] = low_half
    dsend[1] = high_half

    def matrix(n, many=1):
        return ut[pl.ds(pl.multiple_of(64 * n, 64), 64 * many), :]

    def pair(t, n):
        return matrix(2**t - 2 + 2 * n, 2)

    for n in range(16):
        for m in range(2):
            high, low = parts(mm(pair(6, 2 * n + m), matrix(2**5 - 2 + 2 * n + m), NN))
            u_high[n, 128 * m : 128 * m + 128] = high
            u_low[n, 128 * m : 128 * m + 128] = low
    for n in range(4):
        for m in range(2):
            high, low = parts(mm(pair(4, 2 * n + m), matrix(2**3 - 2 + 2 * n + m), NN))
            v_high[n, 128 * m : 128 * m + 128] = high
            v_low[n, 128 * m : 128 * m + 128] = low
    chain = {5: matrix(2**6 - 2 + g)}
    for t in (4, 3, 2, 1, 0):
        chain[t] = mm(chain[t + 1], matrix(2 ** (t + 1) - 2 + g // 2 ** (5 - t)), NN)
    root_part = mm(jnp.zeros((8, 64), F32), chain[0], NT)
    for t in range(2, 6):
        gmap[t - 2, 2] = jnp.concatenate([chain[t], chain[t]], axis=1)
    pl.semaphore_wait(ready_z, 2)
    for k in (1, 2, 3):
        tell(ready_plane, xy(k, 0))

    for c in ld_e:
        c.wait()
    q8 = jnp.concatenate([mm(e10[l], e9[l // 2], NN) for l in range(4)], axis=0)
    q7 = mm(q8, e8[...], NN)
    q6 = mm(q7, e7[...], NN)
    q8s[...] = q8
    q7s[...] = q7
    q6s[...] = q6
    wup[:, 0:128] = jnp.concatenate([q7, q6], axis=1)
    wup[:, 128:256] = jnp.concatenate([q8, q8], axis=1)

    left = left_lanes((8, 128))
    quarter = lax.broadcasted_iota(jnp.int32, (8, 256), 1) // 64
    ld_own.wait()
    ld_basis.wait()
    for c in ins:
        c.wait_recv()
    sent.extend(ins)
    for i in range(16):
        vlf[4 + i] = vin[:, 8 + i, :]

    def climb(p, rows):
        wide = mm(rows, basis[...].reshape(256, 256), NT)
        c10 = jnp.zeros((8, 256), F32)
        for l in range(4):
            c10 = jnp.where(quarter == l, wide[8 * l : 8 * l + 8], c10)
        tops = mm(c10, wup[...], NN)
        xybuf[p, 0, 0] = tops[:, 0:128]
        halo[p][3, 3] = tops[:, 128:256]
        for i, k in XY_ORDER:
            xys[p].append(
                remote(xybuf.at[p, 0, 0], xybuf.at[p, i, k], xy_send.at[p, i, k], xy_recv.at[p, i, k], xy(i, k))
            )
        halo[p][3, 0] = c10[:, 0:128]
        halo[p][3, 1] = c10[:, 128:256]
        halo[p][3, 2] = jnp.concatenate(
            [mm(c10[:, 128 * j : 128 * j + 128], e10[2 * j : 2 * j + 2].reshape(128, 64), NN) for j in range(2)], axis=1
        )
        for k in (1, -1, 2, -2, 3, -3):
            tiles = pl.ds({1: 0, 2: 2, 3: 3}[abs(k)], {1: 4, 2: 2, 3: 1}[abs(k)])
            halos[p].append(
                remote(
                    halo[p].at[3, tiles], halo[p].at[3 - k, tiles], halo_send.at[p, 3 - k], halo_recv.at[p, 3 - k], linear(k)
                )
            )

    xys, halos, ags, c7s = ([], []), ([], []), ([], []), ([], [])

    def near_field(vectors, offset, least):
        def step(s, totals):
            target = pairs[0, s] - 4 * d
            source = jnp.clip(pairs[1, s] - offset, least, least + 11)
            term = mm(vectors[source], near[s], NT)
            return tuple(t + term * jnp.where(target == l, 1.0, 0.0) for l, t in enumerate(totals))

        zero = jnp.zeros((8, 256), F32)
        totals = lax.fori_loop(0, 32, step, (zero,) * 4, unroll=4)
        for l in range(4):
            acc[8 * l : 8 * l + 8] = totals[l]

    def half_of(tile, half):
        return jnp.where(half == 1, swap(tile), tile)[:, 0:64]

    def coupled(blocks, entries, pick):
        total = None
        for k in range(4):
            x = pick(entries[k]) * jnp.where(entries[k] >= 0, 1.0, 0.0)
            term = mm(x, blocks[k], NT)
            total = term if total is None else total + term
        return total

    def local_coupled(p):
        for c in halos[p]:
            c.wait_recv()
        sent.extend(halos[p])

        def pick10(entry):
            at = jnp.clip(entry - 4 * d + 12, 0, 27)
            return half_of(halo[p][at // 4, lax.rem(at, 4) // 2], lax.rem(at, 2))

        def pick9(entry):
            at = jnp.clip(entry - 2 * d + 6, 0, 13)
            return half_of(halo[p][at // 2, 2], lax.rem(at, 2))

        def pick8(entry):
            at = jnp.clip(entry - d + 3, 0, 6)
            return halo[p][at, 3][:, 0:64]

        z10 = [coupled(k10[l], [local_lists[k, 12 + 4 * q + l] for k in range(4)], pick10) for l in range(4)]
        z9 = [coupled(k9[j], [local_lists[k, 4 + 2 * q + j] for k in range(4)], pick9) for j in range(2)]
        z8 = coupled(k8, [local_lists[k, q] for k in range(4)], pick8)
        down = mm(z8, q8s[...], NT)
        below = [mm(z9[j], e10[2 * j : 2 * j + 2].reshape(128, 64), NT) for j in range(2)]
        return down + jnp.concatenate(
            [below[0] + jnp.concatenate(z10[0:2], axis=1), below[1] + jnp.concatenate(z10[2:4], axis=1)], axis=1
        )

    def middle(p):
        for c in xys[p]:
            c.wait_recv()
        sent.extend(xys[p])
        totals = []
        for x in range(4):
            i = lax.rem(gx - x + 4, 4)
            totals.append(xybuf[p, i, 0] + xybuf[p, i, 1] + xybuf[p, i, 2] + xybuf[p, i, 3])
        for j in range(2):
            agsend[p, j] = jnp.where(left, swap(totals[2 * j]), totals[2 * j + 1])
        for i, k in ZC_ORDER:
            ags[p].append(
                remote(agsend.at[p], agbuf.at[p, i, k], ag_send.at[p, i, k], ag_recv.at[p, i, k], zcs(i, k))
            )
        agbuf[p, 0, 0] = agsend[p]

        def own(y):
            return xybuf[p, 0, lax.rem(q - y + 4, 4)]

        c7buf[p][2] = jnp.where(left, own(0) + own(1), swap(own(2) + own(3)))
        for k in (1, -1, 2, -2):
            c7s[p].append(
                remote(c7buf[p].at[2], c7buf[p].at[2 - k], c7_send.at[p, 2 - k], c7_recv.at[p, 2 - k], (group(k), q))
            )

    def middle_coupled(p):
        for c in c7s[p]:
            c.wait_recv()
        sent.extend(c7s[p])

        def pick7(entry):
            at = jnp.clip(entry - 2 * g + 4, 0, 9)
            return half_of(c7buf[p][at // 2], lax.rem(at, 2))

        z7 = coupled(k7, [middle_lists[1 + q // 2, k] for k in range(4)], pick7)
        return mm(z7, q7s[...], NT)

    def share_coupling():
        shares = []
        for t in range(2, 6):
            view = dbuf.at[q, t - 2]
            pltpu.make_async_copy(view, view, d_recv.at[t - 2]).wait()
        for k in (2, 1, 3):
            shares.append(remote(dbuf.at[q], dbuf.at[q], share_send.at[k], share_recv.at[k], xy(0, k)))
        return shares

    def upper_maps(shares):
        for c in shares:
            c.wait_recv()
        sent.extend(shares)
        for t in range(2, 6):
            down = gmap[t - 2, 2][:, 0:64]
            for half in range(2):
                block = jnp.concatenate([dbuf[k, t - 2, half] for k in range(4)], axis=0)
                gmap[t - 2, half] = mm(down, block, NN)
        ld_k[4].wait()
        lower, upper = by_offset(k6, [middle_lists[0, k] for k in range(4)], g)
        gmap[4, 0] = lower
        gmap[4, 1] = upper

    def upper(p):
        for c in ags[p]:
            c.wait_recv()
        sent.extend(ags[p])
        roots = []
        for x in range(2):
            line = []
            for z in range(8):
                zslot = lax.rem(gz - z + 8, 8)
                even = agbuf[p, zslot, gc, x]
                odd = agbuf[p, zslot, 1 - gc, x]
                line.append((jnp.where(left, even, swap(odd)), jnp.where(left, swap(even), odd)))
            roots.extend([a for a, b in line] + [b for a, b in line])
        for i in range(32):
            ctile[16 + i] = roots[i]
        quads = []
        for n in range(16):
            x = jnp.concatenate([roots[2 * n], roots[2 * n + 1]], axis=1)
            quads.append(mm_parts(stacked(x), u_high[n], u_low[n], NN))
        fours = [jnp.concatenate([quads[2 * n], quads[2 * n + 1]], axis=1) for n in range(8)]
        for n in range(8):
            ctile[n] = fours[n]
        total = root_part
        for t in range(2, 7):
            number = g // 2 ** (6 - t)
            for half, offsets in enumerate(((-3, -2), (2, 3))):
                found = []
                for offset in offsets:
                    n = jnp.clip(number + offset, 0, 2**t - 1)
                    if t == 6:
                        c = half_of(ctile[16 + n // 2], lax.rem(n, 2))
                    elif t == 5:
                        c = mm(ctile[16 + n], pair(6, n), NN)
                    elif t == 4:
                        c = half_of(ctile[n // 2], lax.rem(n, 2))
                    elif t == 3:
                        c = mm(ctile[n], pair(4, n), NN)
                    else:
                        x = jnp.concatenate([ctile[2 * n], ctile[2 * n + 1]], axis=1)
                        c = mm_parts(stacked(x), v_high[n], v_low[n], NN)
                    found.append(c)
                total = total + mm(jnp.concatenate(found, axis=1), gmap[t - 2, half], NT)
        return total

    def finish(p, base, w6):
        w10 = base + mm(w6, q6s[...], NT)
        spread = jnp.concatenate([jnp.where(quarter == l, w10, 0.0) for l in range(4)], axis=0)
        rows = mm(spread, basis[...].reshape(256, 256), NN) + acc[...]
        for l in range(4):
            outs[p, l] = rows[8 * l : 8 * l + 8]
        return rows

    rows = jnp.concatenate([vlf[4 + 4 * q + l] for l in range(4)], axis=0)
    pl.semaphore_wait(ready_xy, 3)
    pl.semaphore_wait(ready_group, 2)
    climb(0, rows)
    sent.append(remote(columns.at[:, 8:16], vin.at[pl.ds(2 * q, 2), 0:8], edge_send.at[0], edge_recv.at[0, q], (group(1), 0)))
    sent.append(remote(columns.at[:, 0:8], vin.at[pl.ds(2 * q, 2), 24:32], edge_send.at[1], edge_recv.at[1, q], (group(-1), 3)))
    pl.semaphore_wait(ready_plane, 3)

    def give(i, carry):
        to = first_below + i

        @pl.when(to != g)
        def _():
            remote(dsend, dbuf.at[q, level - 2], d_send.at[i], d_recv.at[level - 2], (to, q))

        @pl.when(to == g)
        def _():
            pltpu.make_async_copy(dsend, dbuf.at[q, level - 2], d_recv.at[level - 2]).start()

        return carry

    lax.fori_loop(0, count, give, 0)


    @pl.when(q == 0)
    def _():
        for k in range(4):
            view = vin.at[2 * k : 2 * k + 2, 0:8]
            pltpu.make_async_copy(view, view, edge_recv.at[0, k]).wait()
        for i in range(4):
            vlf[i] = vin[:, 4 + i, :]

    @pl.when(q == 3)
    def _():
        for k in range(4):
            view = vin.at[2 * k : 2 * k + 2, 24:32]
            pltpu.make_async_copy(view, view, edge_recv.at[1, k]).wait()
        for i in range(4):
            vlf[20 + i] = vin[:, 24 + i, :]

    ld_near.wait()
    near_field(vlf, 16 * g - 4, 4 * q)
    middle(0)
    shares = share_coupling()
    for c in ld_k[:4]:
        c.wait()
    base = local_coupled(0) + middle_coupled(0)
    upper_maps(shares)
    first = finish(0, base, upper(0))
    for l in range(4):
        vnext[4 + l] = first[8 * l : 8 * l + 8]
    vs = [
        remote(vnext.at[4:8], vnext.at[0:4], v_send.at[0], v_recv.at[0], linear(1)),
        remote(vnext.at[4:8], vnext.at[8:12], v_send.at[1], v_recv.at[1], linear(-1)),
    ]
    out0 = pltpu.make_async_copy(outs.at[0], first_hbm, out_sem.at[0])
    out0.start()

    climb(1, first)
    for c in vs:
        c.wait_recv()
    sent.extend(vs)
    near_field(vnext, 4 * d - 4, 0)
    middle(1)
    base = local_coupled(1) + middle_coupled(1)
    finish(1, base, upper(1))
    out1 = pltpu.make_async_copy(outs.at[1], second_hbm, out_sem.at[1])
    out1.start()

    for c in sent:
        c.wait_send()

    def given(i, carry):
        @pl.when(first_below + i != g)
        def _():
            pltpu.make_async_copy(dsend, dsend, d_send.at[i]).wait()

        return carry

    lax.fori_loop(0, count, given, 0)
    out0.wait()
    out1.wait()


def body(
    input_columns,
    near_blocks,
    near_pairs,
    leaf_basis,
    local_transfer,
    local_coupling,
    local_lists,
    middle_transfer,
    middle_coupling,
    middle_lists,
    upper_transfer,
    upper_coupling,
    upper_lists,
):
    smem = pl.BlockSpec(memory_space=pltpu.SMEM)
    anywhere = pl.BlockSpec(memory_space=pl.ANY)
    vm = lambda *shape: pltpu.VMEM(shape, F32)
    dma = lambda *shape: pltpu.SemaphoreType.DMA(shape)
    first, second = pl.pallas_call(
        kernel,
        out_shape=[jax.ShapeDtypeStruct((4, 8, 256), F32)] * 2,
        in_specs=[smem] * 4 + [anywhere] * 9,
        out_specs=[anywhere] * 2,
        scratch_shapes=[
            vm(8, 32, 256), vm(24, 8, 256), vm(12, 8, 256), vm(32, 256, 256), vm(4, 64, 256),
            vm(4, 64, 64), vm(2, 64, 64), vm(64, 64), vm(64, 64),
            vm(4, 4, 64, 64), vm(2, 4, 64, 64), vm(4, 64, 64), vm(4, 64, 64), vm(4, 64, 64),
            vm(64, 64, 126), vm(126 * 64, 64), vm(4, 64, 64),
            vm(2, 16, 128), vm(4, 4, 2, 16, 128),
            pltpu.VMEM((16, 256, 64), BF16), pltpu.VMEM((16, 256, 64), BF16),
            pltpu.VMEM((4, 256, 64), BF16), pltpu.VMEM((4, 256, 64), BF16),
            vm(5, 3, 64, 128), vm(48, 8, 128),
            vm(256, 256), vm(256, 64), vm(256, 64), vm(256, 64),
            vm(7, 4, 8, 128), vm(7, 4, 8, 128), vm(2, 4, 4, 8, 128), vm(2, 2, 8, 128), vm(2, 8, 2, 2, 8, 128),
            vm(5, 8, 128), vm(5, 8, 128), vm(32, 256), vm(2, 4, 8, 256),
            dma(16), dma(4), dma(4), dma(2), dma(2, 4), dma(16), dma(4),
            dma(2, 4, 4), dma(2, 4, 4), dma(2, 7), dma(2, 7), dma(2, 8, 2), dma(2, 8, 2),
            dma(2, 5), dma(2, 5), dma(2), dma(2), dma(2),
            dma(4), dma(4), *[pltpu.SemaphoreType.REGULAR] * 4,
        ],
        compiler_params=pltpu.CompilerParams(
            collective_id=0, has_side_effects=True, vmem_limit_bytes=62 * 2**20
        ),
    )(
        near_pairs.T, local_lists.T, middle_lists, upper_lists,
        input_columns, near_blocks, leaf_basis, local_transfer, local_coupling,
        middle_transfer, middle_coupling, upper_transfer.transpose(1, 2, 0), upper_coupling,
    )
    return (first.transpose(1, 0, 2), second.transpose(1, 0, 2))


def solution(mesh):
    in_specs = (
        P("rhs", "leaf", None),
        P(("leaf", "rhs"), None, None),
        P(("leaf", "rhs"), None),
        P(("leaf", "rhs"), None, None),
        P("leaf", None, None),
        P("leaf", None, None, None),
        P("leaf", None),
        P("leaf", None, None),
        P("leaf", None, None, None),
        P("leaf", None),
        P(),
        P("leaf", None, None, None),
        P("leaf", None),
    )
    out_specs = (P(None, ("leaf", "rhs"), None), P(None, ("leaf", "rhs"), None))
    return jax.shard_map(body, mesh=mesh, in_specs=in_specs, out_specs=out_specs, check_vma=False)
```

```python
import jax
import jax.numpy as jnp
from jax import lax
from jax.experimental import pallas as pl
from jax.experimental.pallas import tpu as pltpu
from jax.sharding import PartitionSpec as P

F32 = jnp.float32
BF16 = jnp.bfloat16
MESH = pl.DeviceIdType.MESH
NN = (((1,), (0,)), ((), ()))
NT = (((1,), (1,)), ((), ()))
XY = [(i, k) for i in range(4) for k in range(4) if (i, k) != (0, 0)]
XY_ORDER = sorted(XY, key=lambda s: -(min(s[0], 4 - s[0]) + min(s[1], 4 - s[1])))
ZC_ORDER = [(4, 0), (4, 1), (3, 0), (3, 1), (5, 0), (5, 1), (2, 0), (2, 1), (6, 0), (6, 1), (1, 0), (1, 1), (7, 0), (7, 1), (0, 1)]
ZC_NEAR = [(2, 0), (2, 1), (6, 0), (6, 1), (1, 0), (1, 1), (7, 0), (7, 1), (0, 1)]


def stacked(x):
    high = x.astype(BF16).astype(F32)
    return jnp.concatenate([high, x - high], axis=0).astype(BF16)


def parts(w):
    high = w.astype(BF16)
    return high, (w - high.astype(F32)).astype(BF16)


def dot(x, w, dims):
    return lax.dot_general(x, w, dims, preferred_element_type=F32)


def mm_parts(xs, high, low, dims):
    y = dot(xs, high, dims) + dot(xs, low, dims)
    rows = xs.shape[0] // 2
    return y[:rows] + y[rows:]


def mm(x, w, dims):
    return mm_parts(stacked(x), *parts(w), dims)


def left_lanes(shape):
    return lax.broadcasted_iota(jnp.int32, shape, len(shape) - 1) < 64


def swap(x):
    return pltpu.roll(x, 64, x.ndim - 1)


def kernel(
    pairs_hbm, local_hbm, middle_hbm, upper_hbm,
    columns, near_hbm, basis_hbm, lt_hbm, lc_hbm, mt_hbm, mc_hbm, ut_hbm, uc_hbm,
    first_hbm, second_hbm,
    vin, vlf, vnext, near, basis, e10, e9, e8, e7, k10, k9, k8, k7, k6, utt, ut, uc,
    dsend, dbuf, u_high, u_low, v_high, v_low, gmap, ctile, wup, q6s, q7s, q8s,
    halo_0, halo_1, xybuf, agsend, agbuf, c7_0, c7_1, acc, outs,
    load_sem, in_send, in_recv, edge_send, edge_recv, d_send, d_recv,
    xy_send, xy_recv, halo_send, halo_recv, ag_send, ag_recv, c7_send, c7_recv, v_send, v_recv, out_sem,
    pairs, local_lists, middle_lists, upper_lists,
    share_send, share_recv, ready_xy, ready_z, ready_group, ready_plane,
):
    halo, c7buf = (halo_0, halo_1), (c7_0, c7_1)
    g = lax.axis_index("leaf")
    q = lax.axis_index("rhs")
    d = 4 * g + q
    gx = g // 16
    zc = lax.rem(g, 16)
    gz, gc = zc // 2, lax.rem(zc, 2)

    def linear(k):
        e = lax.rem(d + k + 256, 256)
        return (e // 4, lax.rem(e, 4))

    def group(k):
        return lax.rem(g + k + 64, 64)

    def xy(i, k):
        return (lax.rem(gx + i, 4) * 16 + zc, lax.rem(q + k, 4))

    def zcs(i, k):
        return (gx * 16 + lax.rem(gz + i, 8) * 2 + lax.rem(gc + k, 2), q)

    level = 2 + (g >= 8).astype(jnp.int32) + (g >= 16).astype(jnp.int32) + (g >= 32).astype(jnp.int32)
    count = jnp.where(g >= 32, 2, jnp.where(g >= 16, 4, jnp.where(g >= 8, 8, jnp.where(g >= 4, 16, 0))))
    start = jnp.where(g >= 32, 32, jnp.where(g >= 16, 16, jnp.where(g >= 8, 8, 4)))
    own_number = g - start
    first_below = own_number * count
    own_inside = jnp.where((g >= first_below) & (g < first_below + count), 1, 0)
    barrier = pltpu.get_barrier_semaphore()

    def greet(device):
        pl.semaphore_signal(barrier, inc=1, device_id=device, device_id_type=MESH)

    for k in (1, 2, 3):
        greet(xy(0, k))
        greet(xy(k, 0))
    for z in ZC_NEAR:
        greet(zcs(*z))
    past = jnp.where(gz == 7, 1 + gc, 0) + jnp.where(gz == 0, 2 - gc, 0)
    for end, core, step in ((7, 1, 1), (0, 0, -1)):
        @pl.when(gz == end)
        def _():
            greet((group(2 * step), q))

        @pl.when((gz == end) & (gc == core))
        def _():
            greet((group(step), q))

    loads = []

    def load(src, dst):
        c = pltpu.make_async_copy(src, dst, load_sem.at[len(loads)])
        c.start()
        loads.append(c)
        return c

    ld_own = load(columns, vin.at[pl.ds(2 * q, 2), 8:24])
    ld_ut = load(ut_hbm, utt)
    ld_lists = [
        load(upper_hbm, upper_lists),
        load(middle_hbm, middle_lists),
        load(local_hbm, local_lists),
        load(pairs_hbm, pairs),
    ]
    ld_e = [
        load(lt_hbm.at[pl.ds(12 + 4 * q, 4)], e10),
        load(lt_hbm.at[pl.ds(4 + 2 * q, 2)], e9),
        load(lt_hbm.at[q], e8),
        load(mt_hbm.at[q // 2], e7),
    ]
    ld_basis = load(basis_hbm, basis)
    ld_uc = load(uc_hbm.at[0], uc)
    ld_k = [
        load(lc_hbm.at[pl.ds(12 + 4 * q, 4)], k10),
        load(lc_hbm.at[pl.ds(4 + 2 * q, 2)], k9),
        load(lc_hbm.at[q], k8),
        load(mc_hbm.at[1 + q // 2], k7),
        load(mc_hbm.at[0], k6),
    ]
    ld_near = load(near_hbm, near)

    pl.semaphore_wait(barrier, 6 + len(ZC_NEAR) + past)

    def tell(semaphore, device):
        pl.semaphore_signal(semaphore, inc=1, device_id=device, device_id_type=MESH)

    def remote(src, dst, ss, rs, device):
        c = pltpu.make_async_remote_copy(
            src_ref=src, dst_ref=dst, send_sem=ss, recv_sem=rs, device_id=device, device_id_type=MESH
        )
        c.start()
        return c

    sent = []
    def give_half(k, half):
        return remote(
            columns.at[:, pl.ds(pl.multiple_of(8 * half, 8), 8)],
            vin.at[pl.ds(2 * q, 2), pl.ds(pl.multiple_of(8 + 8 * half, 8), 8)],
            in_send.at[late, k], in_recv.at[late, k], (g, lax.rem(q + k, 4)),
        )

    ins = []
    for late in range(2):
        for k in (2, 1, 3):
            half = lax.rem(q + k, 4) // 2
            ins.append(give_half(k, half if late == 0 else 1 - half))
    for k in (1, 2, 3):
        tell(ready_xy, xy(k, 0))
    for k in (2, 6):
        tell(ready_z, zcs(k, 0))
    for k in (1, -1):
        tell(ready_group, (group(k), q))

    def by_offset(blocks, entries, number):
        found = []
        for offset in (-3, -2, 2, 3):
            total = None
            for k in range(4):
                weight = jnp.where((entries[k] >= 0) & (entries[k] == number + offset), 1.0, 0.0)
                term = blocks[k] * weight
                total = term if total is None else total + term
            found.append(total)
        return (jnp.concatenate(found[:2], axis=1), jnp.concatenate(found[2:], axis=1))

    ld_ut.wait()
    for a in range(64):
        ut[pl.ds(a, 126, stride=64), :] = utt[a].T
    for c in ld_lists:
        c.wait()
    ld_uc.wait()
    quarter_rows = pl.ds(pl.multiple_of(16 * q, 16), 16)
    low_half, high_half = by_offset(
        [uc[k, quarter_rows, :] for k in range(4)], [upper_lists[0, k] for k in range(4)], own_number
    )
    dsend[0] = low_half
    dsend[1] = high_half

    def matrix(n, many=1):
        return ut[pl.ds(pl.multiple_of(64 * n, 64), 64 * many), :]

    def pair(t, n):
        return matrix(2**t - 2 + 2 * n, 2)

    for n in range(16):
        for m in range(2):
            high, low = parts(mm(pair(6, 2 * n + m), matrix(2**5 - 2 + 2 * n + m), NN))
            u_high[n, 128 * m : 128 * m + 128] = high
            u_low[n, 128 * m : 128 * m + 128] = low
    for n in range(4):
        for m in range(2):
            high, low = parts(mm(pair(4, 2 * n + m), matrix(2**3 - 2 + 2 * n + m), NN))
            v_high[n, 128 * m : 128 * m + 128] = high
            v_low[n, 128 * m : 128 * m + 128] = low
    chain = {5: matrix(2**6 - 2 + g)}
    for t in (4, 3, 2, 1, 0):
        chain[t] = mm(chain[t + 1], matrix(2 ** (t + 1) - 2 + g // 2 ** (5 - t)), NN)
    root_part = mm(jnp.zeros((8, 64), F32), chain[0], NT)
    for t in range(2, 6):
        gmap[t - 2, 2] = jnp.concatenate([chain[t], chain[t]], axis=1)
    pl.semaphore_wait(ready_z, 2)
    for k in (1, 2, 3):
        tell(ready_plane, xy(k, 0))

    for c in ld_e:
        c.wait()
    q8 = jnp.concatenate([mm(e10[l], e9[l // 2], NN) for l in range(4)], axis=0)
    q7 = mm(q8, e8[...], NN)
    q6 = mm(q7, e7[...], NN)
    q8s[...] = q8
    q7s[...] = q7
    q6s[...] = q6
    wup[:, 0:128] = jnp.concatenate([q7, q6], axis=1)
    wup[:, 128:256] = jnp.concatenate([q8, q8], axis=1)

    left = left_lanes((8, 128))
    quarter = lax.broadcasted_iota(jnp.int32, (8, 256), 1) // 64
    ld_own.wait()
    ld_basis.wait()
    for c in ins[:3]:
        c.wait_recv()
    sent.extend(ins)

    def turn(half):
        leaves = vin[:, pl.ds(pl.multiple_of(8 + 8 * half, 8), 8), :]
        for i in range(8):
            vlf[4 + 8 * half + i] = leaves[:, i, :]

    turn(q // 2)

    def climb(p, rows):
        wide = mm(rows, basis[...].reshape(256, 256), NT)
        c10 = jnp.zeros((8, 256), F32)
        for l in range(4):
            c10 = jnp.where(quarter == l, wide[8 * l : 8 * l + 8], c10)
        tops = mm(c10, wup[...], NN)
        xybuf[p, 0, 0] = tops[:, 0:128]
        halo[p][3, 3] = tops[:, 128:256]
        for i, k in XY_ORDER:
            xys[p].append(
                remote(xybuf.at[p, 0, 0], xybuf.at[p, i, k], xy_send.at[p, i, k], xy_recv.at[p, i, k], xy(i, k))
            )
        halo[p][3, 0] = c10[:, 0:128]
        halo[p][3, 1] = c10[:, 128:256]
        halo[p][3, 2] = jnp.concatenate(
            [mm(c10[:, 128 * j : 128 * j + 128], e10[2 * j : 2 * j + 2].reshape(128, 64), NN) for j in range(2)], axis=1
        )
        for k in (1, -1, 2, -2, 3, -3):
            tiles = pl.ds({1: 0, 2: 2, 3: 3}[abs(k)], {1: 4, 2: 2, 3: 1}[abs(k)])
            halos[p].append(
                remote(
                    halo[p].at[3, tiles], halo[p].at[3 - k, tiles], halo_send.at[p, 3 - k], halo_recv.at[p, 3 - k], linear(k)
                )
            )

    xys, halos, ags, c7s = ([], []), ([], []), ([], []), ([], [])

    def near_field(vectors, offset, least):
        def step(s, totals):
            target = pairs[0, s] - 4 * d
            source = jnp.clip(pairs[1, s] - offset, least, least + 11)
            term = mm(vectors[source], near[s], NT)
            return tuple(t + term * jnp.where(target == l, 1.0, 0.0) for l, t in enumerate(totals))

        zero = jnp.zeros((8, 256), F32)
        totals = lax.fori_loop(0, 32, step, (zero,) * 4, unroll=4)
        for l in range(4):
            acc[8 * l : 8 * l + 8] = totals[l]

    def half_of(tile, half):
        return jnp.where(half == 1, swap(tile), tile)[:, 0:64]

    def coupled(blocks, entries, pick):
        total = None
        for k in range(4):
            x = pick(entries[k]) * jnp.where(entries[k] >= 0, 1.0, 0.0)
            term = mm(x, blocks[k], NT)
            total = term if total is None else total + term
        return total

    def local_coupled(p):
        for c in halos[p]:
            c.wait_recv()
        sent.extend(halos[p])

        def pick10(entry):
            at = jnp.clip(entry - 4 * d + 12, 0, 27)
            return half_of(halo[p][at // 4, lax.rem(at, 4) // 2], lax.rem(at, 2))

        def pick9(entry):
            at = jnp.clip(entry - 2 * d + 6, 0, 13)
            return half_of(halo[p][at // 2, 2], lax.rem(at, 2))

        def pick8(entry):
            at = jnp.clip(entry - d + 3, 0, 6)
            return halo[p][at, 3][:, 0:64]

        z10 = [coupled(k10[l], [local_lists[k, 12 + 4 * q + l] for k in range(4)], pick10) for l in range(4)]
        z9 = [coupled(k9[j], [local_lists[k, 4 + 2 * q + j] for k in range(4)], pick9) for j in range(2)]
        z8 = coupled(k8, [local_lists[k, q] for k in range(4)], pick8)
        down = mm(z8, q8s[...], NT)
        below = [mm(z9[j], e10[2 * j : 2 * j + 2].reshape(128, 64), NT) for j in range(2)]
        return down + jnp.concatenate(
            [below[0] + jnp.concatenate(z10[0:2], axis=1), below[1] + jnp.concatenate(z10[2:4], axis=1)], axis=1
        )

    def middle(p):
        for c in xys[p]:
            c.wait_recv()
        sent.extend(xys[p])
        totals = []
        for x in range(4):
            i = lax.rem(gx - x + 4, 4)
            totals.append(xybuf[p, i, 0] + xybuf[p, i, 1] + xybuf[p, i, 2] + xybuf[p, i, 3])
        for j in range(2):
            agsend[p, j] = jnp.where(left, swap(totals[2 * j]), totals[2 * j + 1])
        for i, k in ZC_ORDER:
            ags[p].append(
                remote(agsend.at[p], agbuf.at[p, i, k], ag_send.at[p, i, k], ag_recv.at[p, i, k], zcs(i, k))
            )
        agbuf[p, 0, 0] = agsend[p]

        def own(y):
            return xybuf[p, 0, lax.rem(q - y + 4, 4)]

        c7buf[p][2] = jnp.where(left, own(0) + own(1), swap(own(2) + own(3)))
        for k in (1, -1, 2, -2):
            c7s[p].append(
                remote(c7buf[p].at[2], c7buf[p].at[2 - k], c7_send.at[p, 2 - k], c7_recv.at[p, 2 - k], (group(k), q))
            )

    def middle_coupled(p):
        for c in c7s[p]:
            c.wait_recv()
        sent.extend(c7s[p])

        def pick7(entry):
            at = jnp.clip(entry - 2 * g + 4, 0, 9)
            return half_of(c7buf[p][at // 2], lax.rem(at, 2))

        z7 = coupled(k7, [middle_lists[1 + q // 2, k] for k in range(4)], pick7)
        return mm(z7, q7s[...], NT)

    def share_coupling():
        shares = []
        for t in range(2, 6):
            view = dbuf.at[q, t - 2]
            pltpu.make_async_copy(view, view, d_recv.at[t - 2]).wait()
        for k in (2, 1, 3):
            shares.append(remote(dbuf.at[q], dbuf.at[q], share_send.at[k], share_recv.at[k], xy(0, k)))
        return shares

    def upper_maps(shares):
        for c in shares:
            c.wait_recv()
        sent.extend(shares)
        for t in range(2, 6):
            down = gmap[t - 2, 2][:, 0:64]
            for half in range(2):
                block = jnp.concatenate([dbuf[k, t - 2, half] for k in range(4)], axis=0)
                gmap[t - 2, half] = mm(down, block, NN)
        ld_k[4].wait()
        lower, upper = by_offset(k6, [middle_lists[0, k] for k in range(4)], g)
        gmap[4, 0] = lower
        gmap[4, 1] = upper

    def upper(p):
        for c in ags[p]:
            c.wait_recv()
        sent.extend(ags[p])
        roots = []
        for x in range(2):
            line = []
            for z in range(8):
                zslot = lax.rem(gz - z + 8, 8)
                even = agbuf[p, zslot, gc, x]
                odd = agbuf[p, zslot, 1 - gc, x]
                line.append((jnp.where(left, even, swap(odd)), jnp.where(left, swap(even), odd)))
            roots.extend([a for a, b in line] + [b for a, b in line])
        for i in range(32):
            ctile[16 + i] = roots[i]
        quads = []
        for n in range(16):
            x = jnp.concatenate([roots[2 * n], roots[2 * n + 1]], axis=1)
            quads.append(mm_parts(stacked(x), u_high[n], u_low[n], NN))
        fours = [jnp.concatenate([quads[2 * n], quads[2 * n + 1]], axis=1) for n in range(8)]
        for n in range(8):
            ctile[n] = fours[n]
        total = root_part
        for t in range(2, 7):
            number = g // 2 ** (6 - t)
            for half, offsets in enumerate(((-3, -2), (2, 3))):
                found = []
                for offset in offsets:
                    n = jnp.clip(number + offset, 0, 2**t - 1)
                    if t == 6:
                        c = half_of(ctile[16 + n // 2], lax.rem(n, 2))
                    elif t == 5:
                        c = mm(ctile[16 + n], pair(6, n), NN)
                    elif t == 4:
                        c = half_of(ctile[n // 2], lax.rem(n, 2))
                    elif t == 3:
                        c = mm(ctile[n], pair(4, n), NN)
                    else:
                        x = jnp.concatenate([ctile[2 * n], ctile[2 * n + 1]], axis=1)
                        c = mm_parts(stacked(x), v_high[n], v_low[n], NN)
                    found.append(c)
                total = total + mm(jnp.concatenate(found, axis=1), gmap[t - 2, half], NT)
        return total

    def finish(p, base, w6):
        w10 = base + mm(w6, q6s[...], NT)
        spread = jnp.concatenate([jnp.where(quarter == l, w10, 0.0) for l in range(4)], axis=0)
        rows = mm(spread, basis[...].reshape(256, 256), NN) + acc[...]
        for l in range(4):
            outs[p, l] = rows[8 * l : 8 * l + 8]
        return rows

    rows = jnp.concatenate([vlf[4 + 4 * q + l] for l in range(4)], axis=0)
    pl.semaphore_wait(ready_xy, 3)
    pl.semaphore_wait(ready_group, 2)
    climb(0, rows)
    sent.append(remote(columns.at[:, 8:16], vin.at[pl.ds(2 * q, 2), 0:8], edge_send.at[0], edge_recv.at[0, q], (group(1), 0)))
    sent.append(remote(columns.at[:, 0:8], vin.at[pl.ds(2 * q, 2), 24:32], edge_send.at[1], edge_recv.at[1, q], (group(-1), 3)))
    pl.semaphore_wait(ready_plane, 3)

    def give(i, carry):
        to = first_below + i

        @pl.when(to != g)
        def _():
            remote(dsend, dbuf.at[q, level - 2], d_send.at[i], d_recv.at[level - 2], (to, q))

        @pl.when(to == g)
        def _():
            pltpu.make_async_copy(dsend, dbuf.at[q, level - 2], d_recv.at[level - 2]).start()

        return carry

    lax.fori_loop(0, count, give, 0)


    @pl.when(q == 0)
    def _():
        for k in range(4):
            view = vin.at[2 * k : 2 * k + 2, 0:8]
            pltpu.make_async_copy(view, view, edge_recv.at[0, k]).wait()
        for i in range(4):
            vlf[i] = vin[:, 4 + i, :]

    @pl.when(q == 3)
    def _():
        for k in range(4):
            view = vin.at[2 * k : 2 * k + 2, 24:32]
            pltpu.make_async_copy(view, view, edge_recv.at[1, k]).wait()
        for i in range(4):
            vlf[20 + i] = vin[:, 24 + i, :]

    for c in ins[3:]:
        c.wait_recv()
    turn(1 - q // 2)
    ld_near.wait()
    near_field(vlf, 16 * g - 4, 4 * q)
    middle(0)
    shares = share_coupling()
    for c in ld_k[:4]:
        c.wait()
    base = local_coupled(0) + middle_coupled(0)
    upper_maps(shares)
    first = finish(0, base, upper(0))
    for l in range(4):
        vnext[4 + l] = first[8 * l : 8 * l + 8]
    vs = [
        remote(vnext.at[4:8], vnext.at[0:4], v_send.at[0], v_recv.at[0], linear(1)),
        remote(vnext.at[4:8], vnext.at[8:12], v_send.at[1], v_recv.at[1], linear(-1)),
    ]
    out0 = pltpu.make_async_copy(outs.at[0], first_hbm, out_sem.at[0])
    out0.start()

    climb(1, first)
    for c in vs:
        c.wait_recv()
    sent.extend(vs)
    near_field(vnext, 4 * d - 4, 0)
    middle(1)
    base = local_coupled(1) + middle_coupled(1)
    finish(1, base, upper(1))
    out1 = pltpu.make_async_copy(outs.at[1], second_hbm, out_sem.at[1])
    out1.start()

    for c in sent:
        c.wait_send()

    def given(i, carry):
        @pl.when(first_below + i != g)
        def _():
            pltpu.make_async_copy(dsend, dsend, d_send.at[i]).wait()

        return carry

    lax.fori_loop(0, count, given, 0)
    out0.wait()
    out1.wait()


def body(
    input_columns,
    near_blocks,
    near_pairs,
    leaf_basis,
    local_transfer,
    local_coupling,
    local_lists,
    middle_transfer,
    middle_coupling,
    middle_lists,
    upper_transfer,
    upper_coupling,
    upper_lists,
):
    anywhere = pl.BlockSpec(memory_space=pl.ANY)
    vm = lambda *shape: pltpu.VMEM(shape, F32)
    dma = lambda *shape: pltpu.SemaphoreType.DMA(shape)
    first, second = pl.pallas_call(
        kernel,
        out_shape=[jax.ShapeDtypeStruct((4, 8, 256), F32)] * 2,
        in_specs=[anywhere] * 13,
        out_specs=[anywhere] * 2,
        scratch_shapes=[
            vm(8, 32, 256), vm(24, 8, 256), vm(12, 8, 256), vm(32, 256, 256), vm(4, 64, 256),
            vm(4, 64, 64), vm(2, 64, 64), vm(64, 64), vm(64, 64),
            vm(4, 4, 64, 64), vm(2, 4, 64, 64), vm(4, 64, 64), vm(4, 64, 64), vm(4, 64, 64),
            vm(64, 64, 126), vm(126 * 64, 64), vm(4, 64, 64),
            vm(2, 16, 128), vm(4, 4, 2, 16, 128),
            pltpu.VMEM((16, 256, 64), BF16), pltpu.VMEM((16, 256, 64), BF16),
            pltpu.VMEM((4, 256, 64), BF16), pltpu.VMEM((4, 256, 64), BF16),
            vm(5, 3, 64, 128), vm(48, 8, 128),
            vm(256, 256), vm(256, 64), vm(256, 64), vm(256, 64),
            vm(7, 4, 8, 128), vm(7, 4, 8, 128), vm(2, 4, 4, 8, 128), vm(2, 2, 8, 128), vm(2, 8, 2, 2, 8, 128),
            vm(5, 8, 128), vm(5, 8, 128), vm(32, 256), vm(2, 4, 8, 256),
            dma(20), dma(2, 4), dma(2, 4), dma(2), dma(2, 4), dma(16), dma(4),
            dma(2, 4, 4), dma(2, 4, 4), dma(2, 7), dma(2, 7), dma(2, 8, 2), dma(2, 8, 2),
            dma(2, 5), dma(2, 5), dma(2), dma(2), dma(2),
            pltpu.SMEM((2, 32), jnp.int32), pltpu.SMEM((4, 28), jnp.int32),
            pltpu.SMEM((3, 4), jnp.int32), pltpu.SMEM((1, 4), jnp.int32),
            dma(4), dma(4), *[pltpu.SemaphoreType.REGULAR] * 4,
        ],
        compiler_params=pltpu.CompilerParams(
            collective_id=0, has_side_effects=True, vmem_limit_bytes=62 * 2**20
        ),
    )(
        near_pairs.T, local_lists.T, middle_lists, upper_lists,
        input_columns, near_blocks, leaf_basis, local_transfer, local_coupling,
        middle_transfer, middle_coupling, upper_transfer.transpose(1, 2, 0), upper_coupling,
    )
    return (first.transpose(1, 0, 2), second.transpose(1, 0, 2))


def solution(mesh):
    in_specs = (
        P("rhs", "leaf", None),
        P(("leaf", "rhs"), None, None),
        P(("leaf", "rhs"), None),
        P(("leaf", "rhs"), None, None),
        P("leaf", None, None),
        P("leaf", None, None, None),
        P("leaf", None),
        P("leaf", None, None),
        P("leaf", None, None, None),
        P("leaf", None),
        P(),
        P("leaf", None, None, None),
        P("leaf", None),
    )
    out_specs = (P(None, ("leaf", "rhs"), None), P(None, ("leaf", "rhs"), None))
    return jax.shard_map(body, mesh=mesh, in_specs=in_specs, out_specs=out_specs, check_vma=False)
```

```python
import jax
import jax.numpy as jnp
from jax import lax
from jax.experimental import pallas as pl
from jax.experimental.pallas import tpu as pltpu
from jax.sharding import PartitionSpec as P

F32 = jnp.float32
BF16 = jnp.bfloat16
MESH = pl.DeviceIdType.MESH
NN = (((1,), (0,)), ((), ()))
NT = (((1,), (1,)), ((), ()))
XY = [(i, k) for i in range(4) for k in range(4) if (i, k) != (0, 0)]
XY_ORDER = sorted(XY, key=lambda s: -(min(s[0], 4 - s[0]) + min(s[1], 4 - s[1])))
ZC_ORDER = [(4, 0), (4, 1), (3, 0), (3, 1), (5, 0), (5, 1), (2, 0), (2, 1), (6, 0), (6, 1), (1, 0), (1, 1), (7, 0), (7, 1), (0, 1)]
ZC_NEAR = [(2, 0), (2, 1), (6, 0), (6, 1), (1, 0), (1, 1), (7, 0), (7, 1), (0, 1)]


def stacked(x):
    high = x.astype(BF16).astype(F32)
    return jnp.concatenate([high, x - high], axis=0).astype(BF16)


def parts(w):
    high = w.astype(BF16)
    return high, (w - high.astype(F32)).astype(BF16)


def dot(x, w, dims):
    return lax.dot_general(x, w, dims, preferred_element_type=F32)


def mm_parts(xs, high, low, dims):
    y = dot(xs, high, dims) + dot(xs, low, dims)
    rows = xs.shape[0] // 2
    return y[:rows] + y[rows:]


def mm(x, w, dims):
    return mm_parts(stacked(x), *parts(w), dims)


def left_lanes(shape):
    return lax.broadcasted_iota(jnp.int32, shape, len(shape) - 1) < 64


def swap(x):
    return pltpu.roll(x, 64, x.ndim - 1)


def kernel(
    pairs_hbm, local_hbm, middle_hbm, upper_hbm,
    columns, near_hbm, basis_hbm, lt_hbm, lc_hbm, mt_hbm, mc_hbm, ut_hbm, uc_hbm,
    first_hbm, second_hbm,
    vin, vlf, vnext, near, basis, e10, e9, e8, e7, k10, k9, k8, k7, k6, utt, ut, uc,
    dsend, dbuf, u_high, u_low, v_high, v_low, gmap, ctile, wup, q6s, q7s, q8s,
    halo_0, halo_1, xybuf, agsend, agbuf, c7_0, c7_1, acc, outs,
    load_sem, in_send, in_recv, edge_send, edge_recv, d_send, d_recv,
    xy_send, xy_recv, halo_send, halo_recv, ag_send, ag_recv, c7_send, c7_recv, v_send, v_recv, out_sem,
    pairs, local_lists, middle_lists, upper_lists,
    share_send, share_recv, ready_xy, ready_z, ready_group, ready_plane,
):
    halo, c7buf = (halo_0, halo_1), (c7_0, c7_1)
    g = lax.axis_index("leaf")
    q = lax.axis_index("rhs")
    d = 4 * g + q
    gx = g // 16
    zc = lax.rem(g, 16)
    gz, gc = zc // 2, lax.rem(zc, 2)

    def linear(k):
        e = lax.rem(d + k + 256, 256)
        return (e // 4, lax.rem(e, 4))

    def group(k):
        return lax.rem(g + k + 64, 64)

    def xy(i, k):
        return (lax.rem(gx + i, 4) * 16 + zc, lax.rem(q + k, 4))

    def zcs(i, k):
        return (gx * 16 + lax.rem(gz + i, 8) * 2 + lax.rem(gc + k, 2), q)

    level = 2 + (g >= 8).astype(jnp.int32) + (g >= 16).astype(jnp.int32) + (g >= 32).astype(jnp.int32)
    count = jnp.where(g >= 32, 2, jnp.where(g >= 16, 4, jnp.where(g >= 8, 8, jnp.where(g >= 4, 16, 0))))
    start = jnp.where(g >= 32, 32, jnp.where(g >= 16, 16, jnp.where(g >= 8, 8, 4)))
    own_number = g - start
    first_below = own_number * count
    own_inside = jnp.where((g >= first_below) & (g < first_below + count), 1, 0)
    barrier = pltpu.get_barrier_semaphore()

    def greet(device):
        pl.semaphore_signal(barrier, inc=1, device_id=device, device_id_type=MESH)

    for k in (1, 2, 3):
        greet(xy(0, k))
        greet(xy(k, 0))
    for z in ZC_NEAR:
        greet(zcs(*z))
    past = jnp.where(gz == 7, 1 + gc, 0) + jnp.where(gz == 0, 2 - gc, 0)
    for end, core, step in ((7, 1, 1), (0, 0, -1)):
        @pl.when(gz == end)
        def _():
            greet((group(2 * step), q))

        @pl.when((gz == end) & (gc == core))
        def _():
            greet((group(step), q))

    loads = []

    def load(src, dst):
        c = pltpu.make_async_copy(src, dst, load_sem.at[len(loads)])
        c.start()
        loads.append(c)
        return c

    ld_own = load(columns, vin.at[pl.ds(2 * q, 2), 8:24])
    ld_ut = load(ut_hbm, utt)
    ld_lists = [
        load(upper_hbm, upper_lists),
        load(middle_hbm, middle_lists),
        load(local_hbm, local_lists),
        load(pairs_hbm, pairs),
    ]
    ld_e = [
        load(lt_hbm.at[pl.ds(12 + 4 * q, 4)], e10),
        load(lt_hbm.at[pl.ds(4 + 2 * q, 2)], e9),
        load(lt_hbm.at[q], e8),
        load(mt_hbm.at[q // 2], e7),
    ]
    ld_basis = load(basis_hbm, basis)
    ld_uc = load(uc_hbm.at[0], uc)
    ld_k = [
        load(lc_hbm.at[pl.ds(12 + 4 * q, 4)], k10),
        load(lc_hbm.at[pl.ds(4 + 2 * q, 2)], k9),
        load(lc_hbm.at[q], k8),
        load(mc_hbm.at[1 + q // 2], k7),
        load(mc_hbm.at[0], k6),
    ]
    ld_near = load(near_hbm, near)

    pl.semaphore_wait(barrier, 6 + len(ZC_NEAR) + past)

    def tell(semaphore, device):
        pl.semaphore_signal(semaphore, inc=1, device_id=device, device_id_type=MESH)

    def remote(src, dst, ss, rs, device):
        c = pltpu.make_async_remote_copy(
            src_ref=src, dst_ref=dst, send_sem=ss, recv_sem=rs, device_id=device, device_id_type=MESH
        )
        c.start()
        return c

    sent = []
    def give_half(k, half):
        return remote(
            columns.at[:, pl.ds(pl.multiple_of(8 * half, 8), 8)],
            vin.at[pl.ds(2 * q, 2), pl.ds(pl.multiple_of(8 + 8 * half, 8), 8)],
            in_send.at[late, k], in_recv.at[late, k], (g, lax.rem(q + k, 4)),
        )

    ins = []
    for late in range(2):
        for k in (2, 1, 3):
            half = lax.rem(q + k, 4) // 2
            ins.append(give_half(k, half if late == 0 else 1 - half))
    for k in (1, 2, 3):
        tell(ready_xy, xy(k, 0))
    for k in (2, 6):
        tell(ready_z, zcs(k, 0))
    for k in (1, -1):
        tell(ready_group, (group(k), q))

    def by_offset(blocks, entries, number):
        found = []
        for offset in (-3, -2, 2, 3):
            total = None
            for k in range(4):
                weight = jnp.where((entries[k] >= 0) & (entries[k] == number + offset), 1.0, 0.0)
                term = blocks[k] * weight
                total = term if total is None else total + term
            found.append(total)
        return (jnp.concatenate(found[:2], axis=1), jnp.concatenate(found[2:], axis=1))

    for c in ld_lists:
        c.wait()
    ld_uc.wait()
    quarter_rows = pl.ds(pl.multiple_of(16 * q, 16), 16)
    low_half, high_half = by_offset(
        [uc[k, quarter_rows, :] for k in range(4)], [upper_lists[0, k] for k in range(4)], own_number
    )
    dsend[0] = low_half
    dsend[1] = high_half

    pl.semaphore_wait(ready_z, 2)
    for k in (1, 2, 3):
        tell(ready_plane, xy(k, 0))

    for c in ld_e:
        c.wait()
    q8 = jnp.concatenate([mm(e10[l], e9[l // 2], NN) for l in range(4)], axis=0)
    q7 = mm(q8, e8[...], NN)
    q6 = mm(q7, e7[...], NN)
    q8s[...] = q8
    q7s[...] = q7
    q6s[...] = q6
    wup[:, 0:128] = jnp.concatenate([q7, q6], axis=1)
    wup[:, 128:256] = jnp.concatenate([q8, q8], axis=1)

    left = left_lanes((8, 128))
    quarter = lax.broadcasted_iota(jnp.int32, (8, 256), 1) // 64
    ld_own.wait()
    ld_basis.wait()
    for c in ins[:3]:
        c.wait_recv()
    sent.extend(ins)

    def turn(half):
        leaves = vin[:, pl.ds(pl.multiple_of(8 + 8 * half, 8), 8), :]
        for i in range(8):
            vlf[4 + 8 * half + i] = leaves[:, i, :]

    turn(q // 2)

    def climb(p, rows):
        wide = mm(rows, basis[...].reshape(256, 256), NT)
        c10 = jnp.zeros((8, 256), F32)
        for l in range(4):
            c10 = jnp.where(quarter == l, wide[8 * l : 8 * l + 8], c10)
        tops = mm(c10, wup[...], NN)
        xybuf[p, 0, 0] = tops[:, 0:128]
        halo[p][3, 3] = tops[:, 128:256]
        for i, k in XY_ORDER:
            xys[p].append(
                remote(xybuf.at[p, 0, 0], xybuf.at[p, i, k], xy_send.at[p, i, k], xy_recv.at[p, i, k], xy(i, k))
            )
        halo[p][3, 0] = c10[:, 0:128]
        halo[p][3, 1] = c10[:, 128:256]
        halo[p][3, 2] = jnp.concatenate(
            [mm(c10[:, 128 * j : 128 * j + 128], e10[2 * j : 2 * j + 2].reshape(128, 64), NN) for j in range(2)], axis=1
        )
        for k in (1, -1, 2, -2, 3, -3):
            tiles = pl.ds({1: 0, 2: 2, 3: 3}[abs(k)], {1: 4, 2: 2, 3: 1}[abs(k)])
            halos[p].append(
                remote(
                    halo[p].at[3, tiles], halo[p].at[3 - k, tiles], halo_send.at[p, 3 - k], halo_recv.at[p, 3 - k], linear(k)
                )
            )

    xys, halos, ags, c7s = ([], []), ([], []), ([], []), ([], [])

    def near_field(vectors, offset, least):
        def step(s, totals):
            target = pairs[0, s] - 4 * d
            source = jnp.clip(pairs[1, s] - offset, least, least + 11)
            term = mm(vectors[source], near[s], NT)
            return tuple(t + term * jnp.where(target == l, 1.0, 0.0) for l, t in enumerate(totals))

        zero = jnp.zeros((8, 256), F32)
        totals = lax.fori_loop(0, 32, step, (zero,) * 4, unroll=4)
        for l in range(4):
            acc[8 * l : 8 * l + 8] = totals[l]

    def half_of(tile, half):
        return jnp.where(half == 1, swap(tile), tile)[:, 0:64]

    def coupled(blocks, entries, pick):
        total = None
        for k in range(4):
            x = pick(entries[k]) * jnp.where(entries[k] >= 0, 1.0, 0.0)
            term = mm(x, blocks[k], NT)
            total = term if total is None else total + term
        return total

    def local_coupled(p):
        for c in halos[p]:
            c.wait_recv()
        sent.extend(halos[p])

        def pick10(entry):
            at = jnp.clip(entry - 4 * d + 12, 0, 27)
            return half_of(halo[p][at // 4, lax.rem(at, 4) // 2], lax.rem(at, 2))

        def pick9(entry):
            at = jnp.clip(entry - 2 * d + 6, 0, 13)
            return half_of(halo[p][at // 2, 2], lax.rem(at, 2))

        def pick8(entry):
            at = jnp.clip(entry - d + 3, 0, 6)
            return halo[p][at, 3][:, 0:64]

        z10 = [coupled(k10[l], [local_lists[k, 12 + 4 * q + l] for k in range(4)], pick10) for l in range(4)]
        z9 = [coupled(k9[j], [local_lists[k, 4 + 2 * q + j] for k in range(4)], pick9) for j in range(2)]
        z8 = coupled(k8, [local_lists[k, q] for k in range(4)], pick8)
        down = mm(z8, q8s[...], NT)
        below = [mm(z9[j], e10[2 * j : 2 * j + 2].reshape(128, 64), NT) for j in range(2)]
        return down + jnp.concatenate(
            [below[0] + jnp.concatenate(z10[0:2], axis=1), below[1] + jnp.concatenate(z10[2:4], axis=1)], axis=1
        )

    def middle(p):
        for c in xys[p]:
            c.wait_recv()
        sent.extend(xys[p])
        totals = []
        for x in range(4):
            i = lax.rem(gx - x + 4, 4)
            totals.append(xybuf[p, i, 0] + xybuf[p, i, 1] + xybuf[p, i, 2] + xybuf[p, i, 3])
        for j in range(2):
            agsend[p, j] = jnp.where(left, swap(totals[2 * j]), totals[2 * j + 1])
        for i, k in ZC_ORDER:
            ags[p].append(
                remote(agsend.at[p], agbuf.at[p, i, k], ag_send.at[p, i, k], ag_recv.at[p, i, k], zcs(i, k))
            )
        agbuf[p, 0, 0] = agsend[p]

        def own(y):
            return xybuf[p, 0, lax.rem(q - y + 4, 4)]

        c7buf[p][2] = jnp.where(left, own(0) + own(1), swap(own(2) + own(3)))
        for k in (1, -1, 2, -2):
            c7s[p].append(
                remote(c7buf[p].at[2], c7buf[p].at[2 - k], c7_send.at[p, 2 - k], c7_recv.at[p, 2 - k], (group(k), q))
            )

    def middle_coupled(p):
        for c in c7s[p]:
            c.wait_recv()
        sent.extend(c7s[p])

        def pick7(entry):
            at = jnp.clip(entry - 2 * g + 4, 0, 9)
            return half_of(c7buf[p][at // 2], lax.rem(at, 2))

        z7 = coupled(k7, [middle_lists[1 + q // 2, k] for k in range(4)], pick7)
        return mm(z7, q7s[...], NT)

    def share_coupling():
        shares = []
        for t in range(2, 6):
            view = dbuf.at[q, t - 2]
            pltpu.make_async_copy(view, view, d_recv.at[t - 2]).wait()
        for k in (2, 1, 3):
            shares.append(remote(dbuf.at[q], dbuf.at[q], share_send.at[k], share_recv.at[k], xy(0, k)))
        return shares

    def upper_maps(shares):
        for c in shares:
            c.wait_recv()
        sent.extend(shares)
        for t in range(2, 6):
            down = gmap[t - 2, 2][:, 0:64]
            for half in range(2):
                block = jnp.concatenate([dbuf[k, t - 2, half] for k in range(4)], axis=0)
                gmap[t - 2, half] = mm(down, block, NN)
        ld_k[4].wait()
        lower, upper = by_offset(k6, [middle_lists[0, k] for k in range(4)], g)
        gmap[4, 0] = lower
        gmap[4, 1] = upper

    def upper(p):
        for c in ags[p]:
            c.wait_recv()
        sent.extend(ags[p])
        roots = []
        for x in range(2):
            line = []
            for z in range(8):
                zslot = lax.rem(gz - z + 8, 8)
                even = agbuf[p, zslot, gc, x]
                odd = agbuf[p, zslot, 1 - gc, x]
                line.append((jnp.where(left, even, swap(odd)), jnp.where(left, swap(even), odd)))
            roots.extend([a for a, b in line] + [b for a, b in line])
        for i in range(32):
            ctile[16 + i] = roots[i]
        quads = []
        for n in range(16):
            x = jnp.concatenate([roots[2 * n], roots[2 * n + 1]], axis=1)
            quads.append(mm_parts(stacked(x), u_high[n], u_low[n], NN))
        fours = [jnp.concatenate([quads[2 * n], quads[2 * n + 1]], axis=1) for n in range(8)]
        for n in range(8):
            ctile[n] = fours[n]
        total = root_part
        for t in range(2, 7):
            number = g // 2 ** (6 - t)
            for half, offsets in enumerate(((-3, -2), (2, 3))):
                found = []
                for offset in offsets:
                    n = jnp.clip(number + offset, 0, 2**t - 1)
                    if t == 6:
                        c = half_of(ctile[16 + n // 2], lax.rem(n, 2))
                    elif t == 5:
                        c = mm(ctile[16 + n], pair(6, n), NN)
                    elif t == 4:
                        c = half_of(ctile[n // 2], lax.rem(n, 2))
                    elif t == 3:
                        c = mm(ctile[n], pair(4, n), NN)
                    else:
                        x = jnp.concatenate([ctile[2 * n], ctile[2 * n + 1]], axis=1)
                        c = mm_parts(stacked(x), v_high[n], v_low[n], NN)
                    found.append(c)
                total = total + mm(jnp.concatenate(found, axis=1), gmap[t - 2, half], NT)
        return total

    def finish(p, base, w6):
        w10 = base + mm(w6, q6s[...], NT)
        spread = jnp.concatenate([jnp.where(quarter == l, w10, 0.0) for l in range(4)], axis=0)
        rows = mm(spread, basis[...].reshape(256, 256), NN) + acc[...]
        for l in range(4):
            outs[p, l] = rows[8 * l : 8 * l + 8]
        return rows

    rows = jnp.concatenate([vlf[4 + 4 * q + l] for l in range(4)], axis=0)
    pl.semaphore_wait(ready_xy, 3)
    pl.semaphore_wait(ready_group, 2)
    climb(0, rows)
    sent.append(remote(columns.at[:, 8:16], vin.at[pl.ds(2 * q, 2), 0:8], edge_send.at[0], edge_recv.at[0, q], (group(1), 0)))
    sent.append(remote(columns.at[:, 0:8], vin.at[pl.ds(2 * q, 2), 24:32], edge_send.at[1], edge_recv.at[1, q], (group(-1), 3)))
    pl.semaphore_wait(ready_plane, 3)

    def give(i, carry):
        to = first_below + i

        @pl.when(to != g)
        def _():
            remote(dsend, dbuf.at[q, level - 2], d_send.at[i], d_recv.at[level - 2], (to, q))

        @pl.when(to == g)
        def _():
            pltpu.make_async_copy(dsend, dbuf.at[q, level - 2], d_recv.at[level - 2]).start()

        return carry

    lax.fori_loop(0, count, give, 0)


    ld_ut.wait()
    for a in range(64):
        ut[pl.ds(a, 126, stride=64), :] = utt[a].T
    def matrix(n, many=1):
        return ut[pl.ds(pl.multiple_of(64 * n, 64), 64 * many), :]

    def pair(t, n):
        return matrix(2**t - 2 + 2 * n, 2)

    for n in range(16):
        for m in range(2):
            high, low = parts(mm(pair(6, 2 * n + m), matrix(2**5 - 2 + 2 * n + m), NN))
            u_high[n, 128 * m : 128 * m + 128] = high
            u_low[n, 128 * m : 128 * m + 128] = low
    for n in range(4):
        for m in range(2):
            high, low = parts(mm(pair(4, 2 * n + m), matrix(2**3 - 2 + 2 * n + m), NN))
            v_high[n, 128 * m : 128 * m + 128] = high
            v_low[n, 128 * m : 128 * m + 128] = low
    chain = {5: matrix(2**6 - 2 + g)}
    for t in (4, 3, 2, 1, 0):
        chain[t] = mm(chain[t + 1], matrix(2 ** (t + 1) - 2 + g // 2 ** (5 - t)), NN)
    root_part = mm(jnp.zeros((8, 64), F32), chain[0], NT)
    for t in range(2, 6):
        gmap[t - 2, 2] = jnp.concatenate([chain[t], chain[t]], axis=1)
    @pl.when(q == 0)
    def _():
        for k in range(4):
            view = vin.at[2 * k : 2 * k + 2, 0:8]
            pltpu.make_async_copy(view, view, edge_recv.at[0, k]).wait()
        for i in range(4):
            vlf[i] = vin[:, 4 + i, :]

    @pl.when(q == 3)
    def _():
        for k in range(4):
            view = vin.at[2 * k : 2 * k + 2, 24:32]
            pltpu.make_async_copy(view, view, edge_recv.at[1, k]).wait()
        for i in range(4):
            vlf[20 + i] = vin[:, 24 + i, :]

    for c in ins[3:]:
        c.wait_recv()
    turn(1 - q // 2)
    ld_near.wait()
    middle(0)
    near_field(vlf, 16 * g - 4, 4 * q)
    shares = share_coupling()
    for c in ld_k[:4]:
        c.wait()
    base = local_coupled(0) + middle_coupled(0)
    upper_maps(shares)
    first = finish(0, base, upper(0))
    for l in range(4):
        vnext[4 + l] = first[8 * l : 8 * l + 8]
    vs = [
        remote(vnext.at[4:8], vnext.at[0:4], v_send.at[0], v_recv.at[0], linear(1)),
        remote(vnext.at[4:8], vnext.at[8:12], v_send.at[1], v_recv.at[1], linear(-1)),
    ]
    out0 = pltpu.make_async_copy(outs.at[0], first_hbm, out_sem.at[0])
    out0.start()

    climb(1, first)
    for c in vs:
        c.wait_recv()
    sent.extend(vs)
    near_field(vnext, 4 * d - 4, 0)
    middle(1)
    base = local_coupled(1) + middle_coupled(1)
    finish(1, base, upper(1))
    out1 = pltpu.make_async_copy(outs.at[1], second_hbm, out_sem.at[1])
    out1.start()

    for c in sent:
        c.wait_send()

    def given(i, carry):
        @pl.when(first_below + i != g)
        def _():
            pltpu.make_async_copy(dsend, dsend, d_send.at[i]).wait()

        return carry

    lax.fori_loop(0, count, given, 0)
    out0.wait()
    out1.wait()


def body(
    input_columns,
    near_blocks,
    near_pairs,
    leaf_basis,
    local_transfer,
    local_coupling,
    local_lists,
    middle_transfer,
    middle_coupling,
    middle_lists,
    upper_transfer,
    upper_coupling,
    upper_lists,
):
    anywhere = pl.BlockSpec(memory_space=pl.ANY)
    vm = lambda *shape: pltpu.VMEM(shape, F32)
    dma = lambda *shape: pltpu.SemaphoreType.DMA(shape)
    first, second = pl.pallas_call(
        kernel,
        out_shape=[jax.ShapeDtypeStruct((4, 8, 256), F32)] * 2,
        in_specs=[anywhere] * 13,
        out_specs=[anywhere] * 2,
        scratch_shapes=[
            vm(8, 32, 256), vm(24, 8, 256), vm(12, 8, 256), vm(32, 256, 256), vm(4, 64, 256),
            vm(4, 64, 64), vm(2, 64, 64), vm(64, 64), vm(64, 64),
            vm(4, 4, 64, 64), vm(2, 4, 64, 64), vm(4, 64, 64), vm(4, 64, 64), vm(4, 64, 64),
            vm(64, 64, 126), vm(126 * 64, 64), vm(4, 64, 64),
            vm(2, 16, 128), vm(4, 4, 2, 16, 128),
            pltpu.VMEM((16, 256, 64), BF16), pltpu.VMEM((16, 256, 64), BF16),
            pltpu.VMEM((4, 256, 64), BF16), pltpu.VMEM((4, 256, 64), BF16),
            vm(5, 3, 64, 128), vm(48, 8, 128),
            vm(256, 256), vm(256, 64), vm(256, 64), vm(256, 64),
            vm(7, 4, 8, 128), vm(7, 4, 8, 128), vm(2, 4, 4, 8, 128), vm(2, 2, 8, 128), vm(2, 8, 2, 2, 8, 128),
            vm(5, 8, 128), vm(5, 8, 128), vm(32, 256), vm(2, 4, 8, 256),
            dma(20), dma(2, 4), dma(2, 4), dma(2), dma(2, 4), dma(16), dma(4),
            dma(2, 4, 4), dma(2, 4, 4), dma(2, 7), dma(2, 7), dma(2, 8, 2), dma(2, 8, 2),
            dma(2, 5), dma(2, 5), dma(2), dma(2), dma(2),
            pltpu.SMEM((2, 32), jnp.int32), pltpu.SMEM((4, 28), jnp.int32),
            pltpu.SMEM((3, 4), jnp.int32), pltpu.SMEM((1, 4), jnp.int32),
            dma(4), dma(4), *[pltpu.SemaphoreType.REGULAR] * 4,
        ],
        compiler_params=pltpu.CompilerParams(
            collective_id=0, has_side_effects=True, vmem_limit_bytes=62 * 2**20
        ),
    )(
        near_pairs.T, local_lists.T, middle_lists, upper_lists,
        input_columns, near_blocks, leaf_basis, local_transfer, local_coupling,
        middle_transfer, middle_coupling, upper_transfer.transpose(1, 2, 0), upper_coupling,
    )
    return (first.transpose(1, 0, 2), second.transpose(1, 0, 2))


def solution(mesh):
    in_specs = (
        P("rhs", "leaf", None),
        P(("leaf", "rhs"), None, None),
        P(("leaf", "rhs"), None),
        P(("leaf", "rhs"), None, None),
        P("leaf", None, None),
        P("leaf", None, None, None),
        P("leaf", None),
        P("leaf", None, None),
        P("leaf", None, None, None),
        P("leaf", None),
        P(),
        P("leaf", None, None, None),
        P("leaf", None),
    )
    out_specs = (P(None, ("leaf", "rhs"), None), P(None, ("leaf", "rhs"), None))
    return jax.shard_map(body, mesh=mesh, in_specs=in_specs, out_specs=out_specs, check_vma=False)
```
